512 devices in a mesh: pipe: 8 (over x, core), dp: 64 (over y, z).
Axes of the slice: x: 4, y: 8, z: 8, core: 2. Of those that a mesh axis runs over, the one named last changes fastest.
Arguments:
- acts: bfloat16 [8, 4, 256, 16384], P('pipe', None, None, 'dp'), may hold values from -100 to 100
- act_slot: int32 [8, 4], P('pipe'), may hold values from 0 to 3, each once within a row
- norm_gain: bfloat16 [8, 16384], P('pipe', 'dp'), may hold values from 0.5 to 1.5
- branch_grad: bfloat16 [8, 4, 256, 16384], P('pipe', None, None, 'dp'), may hold values from -6 to 6
- hidden_grad: bfloat16 [8, 4, 256, 53248], P('pipe', None, None, 'dp'), may hold values from -0.29882812 to 0.29882812
- sketch_seed: int32 [8, 53248], P('pipe', 'dp'), may hold values from 1 to 65520
- basis_old: bfloat16 [8, 16384, 256], P('pipe', 'dp'), may hold values from -0.046875 to 0.046875
- moment_old: bfloat16 [8, 256, 53248], P('pipe', None, 'dp'), may hold values from -12 to 12
Outputs:
- input_grad: bfloat16 [8, 4, 256, 16384], P('pipe', None, None, 'dp')
- moment_new: bfloat16 [8, 256, 53248], P('pipe', None, 'dp')
The draws below stay inside these ranges and needn't reach their ends.
Inputs may be any that keep to these rules, and one draw needn't show every extreme that they name: act_slot[s] names each storage slot once.
All inputs are finite; a program needn't handle non-finite values.
Results may differ from the reference program's by a relative error of at most 0.0059.
Values sent between devices are 32-bit elements; how exact they have to be, the bound alone decides.
A program may use at most 64 MiB of HBM per device.

```python
import math
import jax
import jax.numpy as jnp
from jax import lax

D = 16384
FF = 53248
R = 256
MB = 4
TOK = 256
SECTIONS = 8


def draw_acts(key, part):
    first_key, second_key = jax.random.split(jax.random.fold_in(key, 11), 2)
    base = jnp.clip(jax.random.normal(first_key, (SECTIONS, MB, TOK, D), jnp.float32), -4.0, 4.0)
    position = jnp.arange(D, dtype=jnp.float32) / D
    column_scale = jnp.exp(position * math.log(3.0)) * jnp.exp(jax.random.uniform(second_key, (D,), jnp.float32, 0.0, math.log(2.0)))
    values = base * column_scale
    return values.astype(jnp.bfloat16)


def set_ends(array, stream_key, low, top_value):
    extent = array.shape
    index_at = [jax.random.randint(jax.random.fold_in(stream_key, axis), (), 0, extent[axis]) for axis in range(len(extent))]
    array = array.at[tuple(index_at)].set(low)
    longest = extent.index(max(extent))
    index_at[longest] = (index_at[longest] + 1) % extent[longest]
    return array.at[tuple(index_at)].set(top_value)


def level_of(stream_key, dims, cuts, least, top_value):
    level = 1.0
    for dim, blocks in cuts:
        heights = jax.random.uniform(jax.random.fold_in(jax.random.fold_in(stream_key, 6), dim), (blocks,), jnp.float32, least / len(cuts), top_value / len(cuts))
        level = level * jnp.repeat(jnp.exp(heights), dims[dim] // blocks).reshape((-1,) + (1,) * (len(dims) - 1 - dim))
    return level


def bell_draw(own_key, extent, width, most, shards=(), kind=jnp.bfloat16):
    values = jax.random.normal(own_key, extent, jnp.float32) * width
    if len(shards) > 0:
        values = level_of(own_key, extent, shards, -0.22, 0.18) * values
    return jnp.clip(values, min=-most, max=most).astype(kind)


def setup_inputs(seed: int = 0) -> dict:
    keys = jax.random.split(jax.random.key(seed), 9)
    acts = draw_acts(jax.random.fold_in(keys[8], 71), 0)
    act_slot = jax.vmap(lambda own: jax.random.permutation(own, MB))(jax.random.split(keys[1], SECTIONS)).reshape((SECTIONS, MB)).astype(jnp.int32)
    norm_gain = jnp.clip(1.0 + 0.1 * jax.random.normal(keys[2], (SECTIONS, D), jnp.float32), 0.5, 1.5).astype(jnp.bfloat16)
    branch_grad = bell_draw(keys[3], (SECTIONS, MB, TOK, D), 1.0, 6.0, ((0, 8), (3, 64)))
    hidden_grad = bell_draw(keys[4], (SECTIONS, MB, TOK, FF), 0.05, 0.29882812, ((0, 8), (3, 64)))
    sketch_seed = set_ends(jax.random.randint(keys[5], (SECTIONS, FF), 1, 65521), jax.random.fold_in(keys[5], 1), 1, 65520).astype(jnp.int32)
    basis_old = bell_draw(keys[6], (SECTIONS, D, R), D ** -0.5, 0.046875, ((0, 8), (1, 64)))
    moment_old = bell_draw(keys[7], (SECTIONS, R, FF), 2.0, 12.0, ((0, 8), (2, 64)))
    return {"acts": acts, "act_slot": act_slot, "norm_gain": norm_gain, "branch_grad": branch_grad, "hidden_grad": hidden_grad, "sketch_seed": sketch_seed, "basis_old": basis_old, "moment_old": moment_old}


def sketch_table(seed_row):
    columns = jnp.arange(1, R + 1, dtype=jnp.int32)
    levels = seed_row[:, None] * columns[None, :] % 65521
    return ((levels.astype(jnp.float32) - 32760.0) * (1.7320508 / 32760.0)).astype(jnp.bfloat16)

def section_moment(stored, inverse, gain_section, hidden_section, seed_section, basis_section, moment_section):
    highest = lax.Precision.HIGHEST
    gains = gain_section.astype(jnp.float32)
    normed = (stored * inverse * gains).astype(jnp.bfloat16).reshape(MB * TOK, D)
    normed_wide = normed.astype(jnp.float32)
    hidden = hidden_section.reshape(MB * TOK, FF)
    sketched = jnp.dot(hidden.astype(jnp.float32), sketch_table(seed_section).astype(jnp.float32), preferred_element_type=jnp.float32)
    sketch_rows = lax.dot_general(normed_wide, sketched, (((0,), (0,)), ((), ())), precision=highest)
    gram_matrix = jnp.dot(sketch_rows.T, sketch_rows, precision=highest)
    factor = jnp.linalg.cholesky(gram_matrix)
    basis_new = lax.linalg.triangular_solve(factor, sketch_rows, left_side=False, lower=True, transpose_a=True)
    rotation = jnp.dot(basis_new.T, basis_section.astype(jnp.float32), precision=highest)
    projected = jnp.dot(normed_wide, basis_new, precision=highest)
    low_rank = lax.dot_general(projected, hidden.astype(jnp.float32), (((0,), (0,)), ((), ())), precision=highest)
    return (0.9 * jnp.dot(rotation, moment_section.astype(jnp.float32), precision=highest) + 0.1 * low_rank).astype(jnp.bfloat16)

def reference(acts, act_slot, norm_gain, branch_grad, hidden_grad, sketch_seed, basis_old, moment_old):
    stored_list = []
    inverse_list = []
    for section_index in range(SECTIONS):
        stored = acts[section_index][act_slot[section_index].astype(jnp.int32)].astype(jnp.float32)
        inverse = 1.0 / jnp.sqrt(lax.optimization_barrier(jnp.mean(stored * stored, -1, keepdims=True)) + 1e-05)
        stored_list.append(stored)
        inverse_list.append(inverse)
    incoming = jnp.zeros((MB, TOK, D), jnp.float32)
    grads = [None] * SECTIONS
    for section_index in reversed(range(SECTIONS)):
        stored = stored_list[section_index]
        inverse = inverse_list[section_index]
        gains = norm_gain[section_index].astype(jnp.float32)
        upstream = gains * branch_grad[section_index].astype(jnp.float32)
        crossed = lax.optimization_barrier(jnp.mean(stored * upstream, -1, keepdims=True))
        incoming = incoming + inverse * upstream - stored * (inverse * inverse * inverse * crossed)
        grads[section_index] = incoming.astype(jnp.bfloat16)
    moments = []
    for section_index in range(SECTIONS):
        moments.append(section_moment(stored_list[section_index], inverse_list[section_index], norm_gain[section_index], hidden_grad[section_index], sketch_seed[section_index], basis_old[section_index], moment_old[section_index]))
    return (jnp.stack(grads, 0), jnp.stack(moments, 0))
```

```python
import functools

import jax
import jax.numpy as jnp
from jax import lax
from jax.experimental import pallas as pl
from jax.experimental.pallas import tpu as pltpu
from jax.sharding import PartitionSpec as P

D = 16384
R = 256
MESH = pl.DeviceIdType.MESH
HIGHEST = lax.Precision.HIGHEST
PARTS = 2


class Place:
    def __init__(self, side):
        self.side = side
        self.pipe = lax.axis_index("pipe")
        dp = lax.axis_index("dp")
        self.y, self.z = dp // side, dp % side
        self.core = self.pipe % 2
        self.x = self.pipe // 2
        self.turn = 1 - 2 * self.core

    def wrap(self, value):
        return (value + 2 * self.side) % self.side

    def along(self, axis, steps):
        if axis == 0:
            return (self.pipe, self.wrap(self.y + steps) * self.side + self.z)
        return (self.pipe, self.y * self.side + self.wrap(self.z + steps))

    def at(self, axis):
        return self.y if axis == 0 else self.z


def greet(others):
    barrier = pltpu.get_barrier_semaphore()
    for other in others:
        pl.semaphore_signal(barrier, inc=1, device_id=other, device_id_type=MESH)
    pl.semaphore_wait(barrier, len(others))


def send(source, target, send_sem, recv_sem, device):
    copy = pltpu.make_async_remote_copy(
        src_ref=source, dst_ref=target, send_sem=send_sem, recv_sem=recv_sem,
        device_id=device, device_id_type=MESH,
    )
    copy.start()
    return copy


class Reduce:
    def __init__(self, place, x_ref, out_ref, ahead, behind, total, near, sems):
        self.p, self.x, self.out = place, x_ref, out_ref
        self.ahead, self.behind, self.total, self.near = ahead, behind, total, near
        (self.ring_s, self.ring_r, self.near_s, self.near_r,
         self.back_s, self.back_r, self.gather_s, self.gather_r) = sems
        side = place.side
        self.forward, self.backward = side // 2, side // 2 - 1
        self.chunk = x_ref.shape[0] // side
        self.piece = self.chunk // PARTS
        self.sub = self.chunk // side
        self.copies = []

    def cols(self, half):
        return pl.ds(128 * half, 128)

    def rows(self, index, part):
        return pl.ds(pl.multiple_of(index * self.chunk + part * self.piece, 8), self.piece)

    def ring_send(self, half, way, step, part):
        p, steps = self.p, (self.forward, self.backward)[way]
        if step >= steps:
            return
        sign = p.turn if way == 0 else -p.turn
        index = p.wrap(p.at(half) + sign * (steps - step))
        held = (self.ahead, self.behind)[way]
        here = pl.ds(part * self.piece, self.piece)
        own = self.x.at[self.rows(index, part), self.cols(half)]
        if step == 0:
            source = own
        else:
            source = held.at[half, step - 1, here]
            source[...] = source[...] + own[...]
        self.copies.append(send(
            source, held.at[half, step, here],
            self.ring_s.at[half, way, step, part], self.ring_r.at[half, way, step, part],
            p.along(half, sign)))

    def ring_wait(self, half, way, step, part):
        held = (self.ahead, self.behind)[way]
        here = held.at[half, step, pl.ds(part * self.piece, self.piece)]
        pltpu.make_async_copy(here, here, self.ring_r.at[half, way, step, part]).wait()

    def scatter_start(self):
        for part in range(PARTS):
            for half in range(2):
                for way in range(2):
                    self.ring_send(half, way, 0, part)

    def scatter_step(self, step):
        for part in range(PARTS):
            for half in range(2):
                for way in range(2):
                    if step < (self.forward, self.backward)[way]:
                        self.ring_wait(half, way, step, part)
                        self.ring_send(half, way, step + 1, part)

    def near_start(self):
        p = self.p
        for half in range(2):
            mine = pl.ds(pl.multiple_of(p.at(half) * self.chunk, 8), self.chunk)
            self.total[half] = (self.x[mine, self.cols(half)] + self.ahead[half, self.forward - 1]
                                + self.behind[half, self.backward - 1])
            for steps in range(1, p.side):
                there = p.wrap(p.at(1 - half) + steps)
                self.copies.append(send(
                    self.total.at[half, pl.ds(pl.multiple_of(there * self.sub, 8), self.sub)],
                    self.near.at[half, steps - 1],
                    self.near_s.at[half, steps - 1], self.near_r.at[half, steps - 1],
                    p.along(1 - half, steps)))

    def block(self, half):
        p = self.p
        start = p.at(half) * self.chunk + p.at(1 - half) * self.sub
        return pl.ds(pl.multiple_of(start, 8), self.sub)

    def near_end(self):
        p = self.p
        for half in range(2):
            mine = pl.ds(pl.multiple_of(p.at(1 - half) * self.sub, 8), self.sub)
            value = self.total[half, mine]
            for steps in range(1, p.side):
                slot = self.near.at[half, steps - 1]
                pltpu.make_async_copy(slot, slot, self.near_r.at[half, steps - 1]).wait()
                value = value + self.near[half, steps - 1]
            place = self.out.at[self.block(half), self.cols(half)]
            place[...] = value
            for steps in range(1, p.side):
                self.copies.append(send(
                    place, place, self.back_s.at[half, steps - 1], self.back_r.at[half, steps - 1],
                    p.along(1 - half, steps)))

    def back_end(self):
        p = self.p
        for half in range(2):
            for steps in range(1, p.side):
                start = p.at(half) * self.chunk + p.wrap(p.at(1 - half) - steps) * self.sub
                slot = self.out.at[pl.ds(pl.multiple_of(start, 8), self.sub), self.cols(half)]
                pltpu.make_async_copy(slot, slot, self.back_r.at[half, steps - 1]).wait()

    def gather_send(self, half, way, step, part):
        p = self.p
        if step >= (self.forward, self.backward)[way]:
            return
        sign = p.turn if way == 0 else -p.turn
        index = p.wrap(p.at(half) - sign * step)
        place = self.out.at[self.rows(index, part), self.cols(half)]
        self.copies.append(send(
            place, place, self.gather_s.at[half, way, step, part],
            self.gather_r.at[half, way, step, part], p.along(half, sign)))

    def gather_start(self):
        for part in range(PARTS):
            for half in range(2):
                for way in range(2):
                    self.gather_send(half, way, 0, part)

    def gather_step(self, step):
        p = self.p
        for part in range(PARTS):
            for half in range(2):
                for way in range(2):
                    if step < (self.forward, self.backward)[way]:
                        sign = p.turn if way == 0 else -p.turn
                        index = p.wrap(p.at(half) - sign * (step + 1))
                        place = self.out.at[self.rows(index, part), self.cols(half)]
                        pltpu.make_async_copy(
                            place, place, self.gather_r.at[half, way, step, part]).wait()
                        self.gather_send(half, way, step + 1, part)

    def finish(self):
        for copy in self.copies:
            copy.wait_send()


def reduce_scratch(rows, side):
    chunk = rows // side
    dma = pltpu.SemaphoreType.DMA
    return [
        pltpu.VMEM((2, side // 2, chunk, 128), jnp.float32),
        pltpu.VMEM((2, side // 2 - 1, chunk, 128), jnp.float32),
        pltpu.VMEM((2, chunk, 128), jnp.float32),
        pltpu.VMEM((2, side - 1, chunk // side, 128), jnp.float32),
        dma((2, 2, side // 2, PARTS)), dma((2, 2, side // 2, PARTS)),
        dma((2, side - 1)), dma((2, side - 1)),
        dma((2, side - 1)), dma((2, side - 1)),
        dma((2, 2, side // 2, PARTS)), dma((2, 2, side // 2, PARTS)),
    ]


def dp_peers(p):
    return [p.along(axis, steps) for axis in range(2) for steps in range(1, p.side)]


def first_kernel(side, x_ref, stat_ref, out_ref, stat_out, ahead, behind, total, near,
                 a, b, c, d, e, f, g, h, stat_slots, stat_mid, stat_s, stat_r):
    p = Place(side)
    greet(dp_peers(p))
    job = Reduce(p, x_ref, out_ref, ahead, behind, total, near, (a, b, c, d, e, f, g, h))
    copies = []

    def stat_send(source, axis):
        for steps in range(1, side):
            copies.append(send(
                source, stat_slots.at[axis, steps - 1], stat_s.at[axis, steps - 1],
                stat_r.at[axis, steps - 1], p.along(axis, steps)))

    def stat_sum(value, axis):
        for steps in range(1, side):
            slot = stat_slots.at[axis, steps - 1]
            pltpu.make_async_copy(slot, slot, stat_r.at[axis, steps - 1]).wait()
            value = value + stat_slots[axis, steps - 1]
        return value

    stat_send(stat_ref, 0)
    job.scatter_start()
    for step in range(job.forward):
        job.scatter_step(step)
        if step == 1:
            stat_mid[...] = stat_sum(stat_ref[...], 0)
            stat_send(stat_mid, 1)
    job.near_start()
    job.near_end()
    stat_out[...] = stat_sum(stat_mid[...], 1)
    job.back_end()
    job.gather_start()
    for step in range(job.forward):
        job.gather_step(step)
    job.finish()
    for copy in copies:
        copy.wait_send()


def first_reduce(x, stats, side):
    rows = x.shape[0]
    vmem = pl.BlockSpec(memory_space=pltpu.VMEM)
    dma = pltpu.SemaphoreType.DMA
    return pl.pallas_call(
        functools.partial(first_kernel, side),
        out_shape=(jax.ShapeDtypeStruct(x.shape, jnp.float32),
                   jax.ShapeDtypeStruct(stats.shape, jnp.float32)),
        in_specs=[vmem, vmem],
        out_specs=(vmem, vmem),
        scratch_shapes=reduce_scratch(rows, side) + [
            pltpu.VMEM((2, side - 1) + stats.shape, jnp.float32),
            pltpu.VMEM(stats.shape, jnp.float32),
            dma((2, side - 1)), dma((2, side - 1)),
        ],
        compiler_params=pltpu.CompilerParams(collective_id=1, has_side_effects=True),
        name="first_reduce",
    )(x, stats)


CHAIN = 4


def second_kernel(side, chips, x_ref, term_ref, out_ref, g_ref, ahead, behind, total, near,
                  a, b, c, d, e, f, g, h, other, above, pair_s, pair_r, down_s, down_r,
                  give_s, give_r, held):
    p = Place(side)
    dp = p.y * side + p.z
    partner = (p.x * 2 + 1 - p.core, dp)
    upper = (((p.x + 1) % chips) * 2 + p.core, dp)
    lower = (((p.x + chips - 1) % chips) * 2 + p.core, dp)
    greet(dp_peers(p) + [partner, upper, lower])
    job = Reduce(p, x_ref, out_ref, ahead, behind, total, near, (a, b, c, d, e, f, g, h))
    half_rows = term_ref.shape[0] // 2
    size = half_rows // CHAIN

    def rows(core, index):
        return pl.ds(pl.multiple_of(core * half_rows + index * size, 8), size)

    def pair_copy(index):
        here = pl.ds(pl.multiple_of(index * size, 8), size)
        return pltpu.make_async_remote_copy(
            src_ref=term_ref.at[rows(1 - p.core, index)], dst_ref=other.at[here],
            send_sem=pair_s.at[index], recv_sem=pair_r.at[index],
            device_id=partner, device_id_type=MESH)

    def down_copy(index):
        here = pl.ds(pl.multiple_of(index * size, 8), size)
        return pltpu.make_async_remote_copy(
            src_ref=held.at[here], dst_ref=above.at[here],
            send_sem=down_s.at[index], recv_sem=down_r.at[index],
            device_id=lower, device_id_type=MESH)

    def give_copy(index):
        place = g_ref.at[rows(p.core, index)]
        here = pl.ds(pl.multiple_of(half_rows + index * size, 8), size)
        return pltpu.make_async_remote_copy(
            src_ref=held.at[here], dst_ref=place,
            send_sem=give_s.at[index], recv_sem=give_r.at[index],
            device_id=partner, device_id_type=MESH)

    def chain_slot(slot):
        for shift in range(chips):
            index = slot - shift
            if 0 <= index < CHAIN:
                @pl.when(p.x == chips - 1 - shift)
                def _():
                    here = pl.ds(index * size, size)
                    pair_copy(index).wait_recv()
                    own = term_ref[rows(p.core, index)]
                    mate = other[here]
                    if shift > 0:
                        down_copy(index).wait_recv()
                        own_sum = own + above[here]
                        mate_sum = mate + above[here]
                    else:
                        own_sum, mate_sum = own, mate
                    both = own_sum + mate
                    lead = p.core == 0
                    held[here] = both
                    held[pl.ds(half_rows + index * size, size)] = jnp.where(lead, mate_sum, both)
                    g_ref[rows(p.core, index)] = jnp.where(lead, both, own_sum)
                    if shift < chips - 1:
                        down_copy(index).start()
                    give_copy(index).start()

    for index in range(CHAIN):
        pair_copy(index).start()
    job.scatter_start()
    for step in range(job.forward):
        job.scatter_step(step)
        chain_slot(step)
    job.near_start()
    chain_slot(4)
    job.near_end()
    chain_slot(5)
    job.back_end()
    job.gather_start()
    chain_slot(6)
    for step in range(job.forward):
        job.gather_step(step)
    for index in range(CHAIN):
        pair_copy(index).wait_send()
        give_copy(index).wait_send()
        place = g_ref.at[rows(1 - p.core, index)]
        pltpu.make_async_copy(place, place, give_r.at[index]).wait()

    @pl.when(p.x > 0)
    def _():
        for index in range(CHAIN):
            down_copy(index).wait_send()

    job.finish()


def second_reduce(x, term, side, chips):
    rows = x.shape[0]
    vmem = pl.BlockSpec(memory_space=pltpu.VMEM)
    dma = pltpu.SemaphoreType.DMA
    half = (term.shape[0] // 2, term.shape[1])
    return pl.pallas_call(
        functools.partial(second_kernel, side, chips),
        out_shape=(jax.ShapeDtypeStruct(x.shape, jnp.float32),
                   jax.ShapeDtypeStruct(term.shape, jnp.float32)),
        in_specs=[vmem, vmem],
        out_specs=(vmem, vmem),
        scratch_shapes=reduce_scratch(rows, side) + [
            pltpu.VMEM(half, jnp.float32), pltpu.VMEM(half, jnp.float32),
            dma((CHAIN,)), dma((CHAIN,)), dma((CHAIN,)), dma((CHAIN,)),
            dma((CHAIN,)), dma((CHAIN,)),
            pltpu.VMEM(term.shape, jnp.float32),
        ],
        compiler_params=pltpu.CompilerParams(collective_id=2, has_side_effects=True),
        name="second_reduce",
    )(x, term)


PANEL = 32


def factor_kernel(gram_ref, inverse_ref, upper, work):
    width = PANEL
    row = lax.broadcasted_iota(jnp.int32, (width, 128), 0)
    lane = lax.broadcasted_iota(jnp.int32, (width, 128), 1)
    for panel in range(R // width):
        start = panel * width
        here = pl.ds(start, width)
        block = gram_ref[here, :]
        wide = lax.broadcasted_iota(jnp.int32, (width, R), 1)
        deep = lax.broadcasted_iota(jnp.int32, (width, R), 0)
        target = jnp.where(wide == deep + start, 1.0, 0.0).astype(jnp.float32)
        if panel > 0:
            left = upper[pl.ds(0, start), :][:, start:start + width]
            block = block - lax.dot_general(left, upper[pl.ds(0, start), :], (((0,), (0,)), ((), ())),
                                            precision=HIGHEST, preferred_element_type=jnp.float32)
            target = target - lax.dot_general(left, inverse_ref[pl.ds(0, start), :],
                                              (((0,), (0,)), ((), ())), precision=HIGHEST,
                                              preferred_element_type=jnp.float32)
        tile = block[:, start:start + width]
        work[...] = jnp.where(lane == row + width, 1.0, 0.0).astype(jnp.float32)
        work[:, 0:width] = tile
        value = work[...]
        for k in range(width):
            column = jnp.broadcast_to(value[:, k:k + 1], (width, 128))
            scale = lax.rsqrt(column[k:k + 1, :])
            pivot_row = value[k:k + 1, :] * scale
            weights = jnp.where(row > k, column, 0.0) * scale
            value = jnp.where(row == k, pivot_row, value - weights * pivot_row)
        corner = value[:, width:2 * width]
        upper[here, :] = jnp.dot(corner, block, precision=HIGHEST, preferred_element_type=jnp.float32)
        inverse_ref[here, :] = jnp.dot(corner, target, precision=HIGHEST,
                                       preferred_element_type=jnp.float32)


def factor_inverse(gram):
    vmem = pl.BlockSpec(memory_space=pltpu.VMEM)
    return pl.pallas_call(
        factor_kernel,
        out_shape=jax.ShapeDtypeStruct((R, R), jnp.float32),
        in_specs=[vmem],
        out_specs=vmem,
        scratch_shapes=[pltpu.VMEM((R, R), jnp.float32), pltpu.VMEM((PANEL, 128), jnp.float32)],
        name="factor_inverse",
    )(gram)


def sketch_table(seed_row):
    columns = jnp.arange(1, R + 1, dtype=jnp.int32)
    levels = seed_row[:, None] * columns[None, :] % 65521
    return ((levels.astype(jnp.float32) - 32760.0) * (1.7320508 / 32760.0)).astype(jnp.bfloat16)


def local(side, acts, act_slot, norm_gain, branch_grad, hidden_grad, sketch_seed, basis_old, moment_old):
    stored = acts[0][act_slot[0]].astype(jnp.float32)
    gains = norm_gain[0].astype(jnp.float32)
    upstream = gains * branch_grad[0].astype(jnp.float32)
    features = stored.shape[-1]
    tokens = stored.shape[0] * stored.shape[1]
    squares_part = jnp.sum(stored * stored, -1).reshape(-1, 128)
    crossed_part = jnp.sum(stored * upstream, -1).reshape(-1, 128)
    hidden = hidden_grad[0].reshape(tokens, -1)
    sketch_part = jnp.dot(hidden, sketch_table(sketch_seed[0]), preferred_element_type=jnp.float32)
    sketched, stats = first_reduce(
        sketch_part, jnp.concatenate([squares_part, crossed_part], 0), side)
    shape = stored.shape[:-1] + (1,)
    squares = stats[:tokens // 128].reshape(shape)
    inverse = 1.0 / jnp.sqrt(squares / D + 1e-05)
    crossed = stats[tokens // 128:].reshape(shape) / D
    term = inverse * upstream - stored * (inverse * inverse * inverse * crossed)
    normed = (stored * inverse * gains).astype(jnp.bfloat16).reshape(tokens, features)
    normed_wide = normed.astype(jnp.float32)
    sketch_rows = lax.dot_general(
        normed_wide, sketched, (((0,), (0,)), ((), ())), precision=HIGHEST)
    stacked = jnp.concatenate(
        [normed_wide, basis_old[0].astype(jnp.float32).T, sketch_rows.T], 0)
    parts = jnp.dot(stacked, sketch_rows, precision=HIGHEST)
    chips = lax.axis_size("pipe") // 2
    sums, grad = second_reduce(parts, term.reshape(tokens, features), side, chips)
    input_grad = grad.astype(jnp.bfloat16).reshape(branch_grad.shape)
    pushed, cross, gram = sums[:tokens], sums[tokens:tokens + R], sums[tokens + R:]
    factor_inv = factor_inverse(gram)
    mixed = 0.9 * lax.dot_general(
        cross, moment_old[0].astype(jnp.float32), (((0,), (0,)), ((), ())), precision=HIGHEST
    ) + 0.1 * lax.dot_general(
        pushed, hidden.astype(jnp.float32), (((0,), (0,)), ((), ())), precision=HIGHEST)
    moment_new = jnp.dot(factor_inv, mixed, precision=HIGHEST).astype(jnp.bfloat16)
    return (input_grad, moment_new[None])


def solution(mesh):
    in_specs = (
        P("pipe", None, None, "dp"),
        P("pipe", None),
        P("pipe", "dp"),
        P("pipe", None, None, "dp"),
        P("pipe", None, None, "dp"),
        P("pipe", "dp"),
        P("pipe", "dp", None),
        P("pipe", None, "dp"),
    )
    out_specs = (P("pipe", None, None, "dp"), P("pipe", None, "dp"))
    side = int(round(mesh.shape["dp"] ** 0.5))
    return jax.shard_map(functools.partial(local, side), mesh=mesh, in_specs=in_specs,
                         out_specs=out_specs, check_vma=False)
```

```python
import functools

import jax
import jax.numpy as jnp
from jax import lax
from jax.experimental import pallas as pl
from jax.experimental.pallas import tpu as pltpu
from jax.sharding import PartitionSpec as P

D = 16384
R = 256
MESH = pl.DeviceIdType.MESH
HIGHEST = lax.Precision.HIGHEST
F32 = jnp.float32
BF16 = jnp.bfloat16
SIDE = 8
CHAIN = 4
PANEL = 32
FIRST = ((0,), (0,))
LAST = ((1,), (1,))
PLAIN = ((1,), (0,))


def dot(a, b, contract=PLAIN, precision=None):
    return lax.dot_general(a, b, (contract, ((), ())), precision=precision,
                           preferred_element_type=F32)


def split(value, count):
    parts = []
    for _ in range(count):
        part = value.astype(BF16)
        parts.append(part)
        value = value - part.astype(F32)
    return parts


class Place:
    def __init__(self):
        self.pipe = lax.axis_index("pipe")
        self.dp = lax.axis_index("dp")
        self.y, self.z = self.dp // SIDE, self.dp % SIDE
        self.core = self.pipe % 2
        self.x = self.pipe // 2
        self.turn = 1 - 2 * self.core

    def wrap(self, value):
        return (value + 2 * SIDE) % SIDE

    def along(self, axis, steps):
        if axis == 0:
            return (self.pipe, self.wrap(self.y + steps) * SIDE + self.z)
        return (self.pipe, self.y * SIDE + self.wrap(self.z + steps))

    def at(self, axis):
        return self.y if axis == 0 else self.z


def send(source, target, send_sem, recv_sem, device):
    pltpu.make_async_remote_copy(
        src_ref=source, dst_ref=target, send_sem=send_sem, recv_sem=recv_sem,
        device_id=device, device_id_type=MESH,
    ).start()


def await_bytes(like, sem):
    pltpu.make_async_copy(like, like, sem).wait()


class Reduce:
    def __init__(self, place, x, out, scratch):
        self.p, self.x, self.out = place, x, out
        self.tree, self.total, self.near, self.recv, self.sent = scratch
        self.chunk = x.shape[0] // SIDE
        self.sub = self.chunk // SIDE

    @staticmethod
    def scratch(rows):
        chunk = rows // SIDE
        return [
            pltpu.VMEM((2, 7, chunk, 128), F32),
            pltpu.VMEM((2, chunk, 128), F32),
            pltpu.VMEM((2, SIDE - 1, chunk // SIDE, 128), F32),
            pltpu.SemaphoreType.DMA((2, 8)),
            pltpu.SemaphoreType.DMA((2, 4)),
        ]

    def part(self, ref, half, index):
        rows = pl.ds(pl.multiple_of(index * self.chunk, 8), self.chunk)
        return ref.at[rows, pl.ds(128 * half, 128)]

    def owned(self, half, steps):
        p = self.p
        return p.wrap(p.at(half) + p.turn * steps)

    def tree_send(self, half, source, slot, sem, steps):
        p = self.p
        send(source, self.tree.at[half, slot], self.sent.at[half, 0], self.recv.at[half, sem],
             p.along(half, p.turn * steps))

    def scatter_start(self):
        for owner, slot, sem, steps in ((4, 0, 0, 2), (3, 1, 0, 1), (-3, 2, 1, -1),
                                        (1, 3, 2, 1), (-1, 4, 2, -1)):
            for half in range(2):
                self.tree_send(half, self.part(self.x, half, self.owned(half, owner)),
                               slot, sem, steps)

    def scatter_mid(self):
        for half in range(2):
            await_bytes(self.tree.at[half, 0:2], self.recv.at[half, 0])
            self.tree[half, 0] = (self.tree[half, 0] + self.tree[half, 1]
                                  + self.part(self.x, half, self.owned(half, 2))[...])
            self.tree_send(half, self.tree.at[half, 0], 5, 2, 2)
        for half in range(2):
            await_bytes(self.tree.at[half, 2], self.recv.at[half, 1])
            self.tree[half, 2] = (self.tree[half, 2]
                                  + self.part(self.x, half, self.owned(half, -2))[...])
            self.tree_send(half, self.tree.at[half, 2], 6, 2, -2)

    def scatter_end(self):
        p = self.p
        for half in range(2):
            await_bytes(self.tree.at[half, 3:7], self.recv.at[half, 2])
            value = self.part(self.x, half, p.at(half))[...]
            for slot in range(3, 7):
                value = value + self.tree[half, slot]
            self.total[half] = value
            for steps in (4, 3, 5, 2, 6, 1, 7):
                there = p.wrap(p.at(1 - half) + steps)
                send(self.total.at[half, pl.ds(pl.multiple_of(there * self.sub, 8), self.sub)],
                     self.near.at[half, steps - 1], self.sent.at[half, 1],
                     self.recv.at[half, 3], p.along(1 - half, steps))

    def near_end(self):
        p = self.p
        for half in range(2):
            await_bytes(self.near.at[half], self.recv.at[half, 3])
            value = self.total[half, pl.ds(pl.multiple_of(p.at(1 - half) * self.sub, 8), self.sub)]
            for slot in range(SIDE - 1):
                value = value + self.near[half, slot]
            start = p.at(half) * self.chunk + p.at(1 - half) * self.sub
            place = self.out.at[pl.ds(pl.multiple_of(start, 8), self.sub), pl.ds(128 * half, 128)]
            place[...] = value
            for steps in (4, 3, 5, 2, 6, 1, 7):
                send(place, place, self.sent.at[half, 2], self.recv.at[half, 4],
                     p.along(1 - half, steps))

    def gather_send(self, half, index, sem, steps):
        p = self.p
        place = self.part(self.out, half, index)
        send(place, place, self.sent.at[half, 3], self.recv.at[half, sem],
             p.along(half, p.turn * steps))

    def gather_start(self):
        for half in range(2):
            await_bytes(self.near.at[half], self.recv.at[half, 4])
            for sem, steps in ((5, 2), (6, -2), (7, 1), (7, -1)):
                self.gather_send(half, self.p.at(half), sem, steps)

    def gather_mid(self):
        for half in range(2):
            await_bytes(self.tree.at[half, 0], self.recv.at[half, 5])
            self.gather_send(half, self.owned(half, -2), 7, 2)
            self.gather_send(half, self.owned(half, -2), 7, 1)
        for half in range(2):
            await_bytes(self.tree.at[half, 0], self.recv.at[half, 6])
            self.gather_send(half, self.owned(half, 2), 7, -1)

    def gather_end(self):
        for half in range(2):
            await_bytes(self.tree.at[half, 0:5], self.recv.at[half, 7])

    def finish(self):
        for half in range(2):
            await_bytes(self.tree.at[half], self.sent.at[half, 0])
            await_bytes(self.near.at[half], self.sent.at[half, 1])
            await_bytes(self.near.at[half], self.sent.at[half, 2])
            await_bytes(self.tree.at[half], self.sent.at[half, 3])


class Small:
    def __init__(self, place, x, out, scratch):
        self.p, self.x, self.out = place, x, out
        self.slots, self.mid, self.recv, self.sent = scratch
        self.chunk = x.shape[0] // SIDE

    @staticmethod
    def scratch(rows):
        chunk = rows // SIDE
        return [
            pltpu.VMEM((2, 2, SIDE - 1, chunk, 128), F32),
            pltpu.VMEM((2, chunk, 128), F32),
            pltpu.SemaphoreType.DMA((2, 3)),
            pltpu.SemaphoreType.DMA((2, 3)),
        ]

    def part(self, ref, half, index):
        rows = pl.ds(pl.multiple_of(index * self.chunk, 8), self.chunk)
        return ref.at[rows, pl.ds(128 * half, 128)]

    def start(self):
        p = self.p
        for steps in (4, 3, 5, 2, 6, 1, 7):
            for half in range(2):
                send(self.part(self.x, half, p.wrap(p.at(half) + steps)),
                     self.slots.at[0, half, steps - 1], self.sent.at[half, 0],
                     self.recv.at[half, 0], p.along(half, steps))

    def total(self, stage, half, value):
        await_bytes(self.slots.at[stage, half], self.recv.at[half, stage])
        for slot in range(SIDE - 1):
            value = value + self.slots[stage, half, slot]
        return value

    def middle(self):
        p = self.p
        for half in range(2):
            self.mid[half] = self.total(0, half, self.part(self.x, half, p.at(half))[...])
            for steps in (4, 3, 5, 2, 6, 1, 7):
                send(self.mid.at[half], self.slots.at[1, half, steps - 1], self.sent.at[half, 1],
                     self.recv.at[half, 1], p.along(1 - half, steps))

    def spread(self):
        p = self.p
        for half in range(2):
            place = self.part(self.out, half, p.at(half))
            place[...] = self.total(1, half, self.mid[half])
            for steps in (4, 3, 5, 2, 6, 1, 7):
                send(place, place, self.sent.at[half, 2], self.recv.at[half, 2],
                     p.along(half, steps))

    def end(self):
        for half in range(2):
            await_bytes(self.slots.at[0, half], self.recv.at[half, 2])

    def finish(self):
        for half in range(2):
            for stage in range(3):
                await_bytes(self.slots.at[0, half], self.sent.at[half, stage])


class Stats:
    def __init__(self, place, tile, slots, mid, recv, sent):
        self.p, self.tile, self.slots, self.mid = place, tile, slots, mid
        self.recv, self.sent = recv, sent

    def push(self, source, axis):
        for steps in (4, 3, 5, 2, 6, 1, 7):
            send(source, self.slots.at[axis, steps - 1], self.sent.at[axis], self.recv.at[axis],
                 self.p.along(axis, steps))

    def total(self, source, axis):
        await_bytes(self.slots.at[axis], self.recv.at[axis])
        value = source[...]
        for slot in range(SIDE - 1):
            value = value + self.slots[axis, slot]
        return value

    def start(self):
        self.push(self.tile, 0)

    def middle(self):
        self.mid[...] = self.total(self.tile, 0)
        self.push(self.mid, 1)

    def end(self):
        return self.total(self.mid, 1)

    def finish(self):
        for axis in range(2):
            await_bytes(self.slots.at[axis], self.sent.at[axis])


class Chain:
    def __init__(self, place, chips, term, grad, other, above, held, sems):
        self.p, self.chips = place, chips
        self.term, self.grad, self.other, self.above, self.held = term, grad, other, above, held
        self.pair_s, self.pair_r, self.down_s, self.down_r, self.give_s, self.give_r = sems
        self.half_rows = term.shape[0] // 2
        self.size = self.half_rows // CHAIN
        self.partner, self.upper, self.lower = chain_peers(place, chips)

    def rows(self, core, index):
        return pl.ds(pl.multiple_of(core * self.half_rows + index * self.size, 8), self.size)

    def remote(self, source, target, send_sem, recv_sem, device):
        return pltpu.make_async_remote_copy(
            src_ref=source, dst_ref=target, send_sem=send_sem, recv_sem=recv_sem,
            device_id=device, device_id_type=MESH)

    def pair(self, index):
        here = pl.ds(index * self.size, self.size)
        return self.remote(self.term.at[self.rows(1 - self.p.core, index)], self.other.at[here],
                           self.pair_s.at[index], self.pair_r.at[index], self.partner)

    def down(self, index):
        here = pl.ds(index * self.size, self.size)
        return self.remote(self.held.at[here], self.above.at[here],
                           self.down_s.at[index], self.down_r.at[index], self.lower)

    def give(self, index):
        here = pl.ds(self.half_rows + index * self.size, self.size)
        return self.remote(self.held.at[here], self.grad.at[self.rows(self.p.core, index)],
                           self.give_s.at[index], self.give_r.at[index], self.partner)

    def start(self):
        for index in range(CHAIN):
            self.pair(index).start()

    def slot(self, slot):
        for shift in range(self.chips):
            index = slot - shift
            if 0 <= index < CHAIN:
                @pl.when(self.p.x == self.chips - 1 - shift)
                def _():
                    here = pl.ds(index * self.size, self.size)
                    self.pair(index).wait_recv()
                    own_sum = self.term[self.rows(self.p.core, index)]
                    mate = self.other[here]
                    mate_sum = mate
                    if shift > 0:
                        self.down(index).wait_recv()
                        own_sum = own_sum + self.above[here]
                        mate_sum = mate + self.above[here]
                    both = own_sum + mate
                    lead = self.p.core == 0
                    self.held[here] = both
                    self.held[pl.ds(self.half_rows + index * self.size, self.size)] = jnp.where(
                        lead, mate_sum, both)
                    self.grad[self.rows(self.p.core, index)] = jnp.where(lead, both, own_sum)
                    if shift < self.chips - 1:
                        self.down(index).start()
                    self.give(index).start()

    def end(self):
        for index in range(CHAIN):
            place = self.grad.at[self.rows(1 - self.p.core, index)]
            await_bytes(place, self.give_r.at[index])

    def finish(self):
        for index in range(CHAIN):
            self.pair(index).wait_send()
            self.give(index).wait_send()

        @pl.when(self.p.x > 0)
        def _():
            for index in range(CHAIN):
                self.down(index).wait_send()


def chain_peers(p, chips):
    return ((p.x * 2 + 1 - p.core, p.dp),
            (((p.x + 1) % chips) * 2 + p.core, p.dp),
            (((p.x + chips - 1) % chips) * 2 + p.core, p.dp))


def factor_panel(panel, gram, inverse, upper):
    width = PANEL
    start = panel * width
    here = pl.ds(start, width)
    row = lax.broadcasted_iota(jnp.int32, (width, 128), 0)
    lane = lax.broadcasted_iota(jnp.int32, (width, 128), 1)
    block = gram[here, :]
    wide = lax.broadcasted_iota(jnp.int32, (width, R), 1)
    deep = lax.broadcasted_iota(jnp.int32, (width, R), 0)
    target = jnp.where(wide == deep + start, 1.0, 0.0).astype(F32)
    if panel > 0:
        before = upper[0:start, :]
        left = before[:, start:start + width]
        block = block - dot(left, before, FIRST, HIGHEST)
        target = target - dot(left, inverse[0:start, :], FIRST, HIGHEST)
    tile = block[:, 128 * (start // 128):128 * (start // 128) + 128]
    shift = start % 128
    if shift:
        tile = pltpu.roll(tile, 128 - shift, 1)
    value = jnp.where(lane < width, tile, jnp.where(lane == row + width, 1.0, 0.0).astype(F32))
    for k in range(width):
        column = jnp.broadcast_to(value[:, k:k + 1], (width, 128))
        scale = lax.rsqrt(column[k:k + 1, :])
        pivot_row = value[k:k + 1, :] * scale
        weights = jnp.where(row > k, column, 0.0) * scale
        value = jnp.where(row == k, pivot_row, value - weights * pivot_row)
    corner = value[:, width:2 * width]
    upper[here, :] = dot(corner, block, PLAIN, HIGHEST)
    inverse[here, :] = dot(corner, target, PLAIN, HIGHEST)


def kernel(chips, acts, slots, gain, branch, hidden, seed, basis, moment, grad_out, moment_out,
           stored, part_s, sum_s, normed, term, grad, part_q, sum_q, part_g, sum_g, part_c, sum_c,
           inverse, upper, stat_tile, stat_slots, stat_mid, stat_recv, stat_sent,
           other, above, held, *rest):
    rest = list(rest)
    chain_sems = [rest.pop(0) for _ in range(6)]
    scratch = [[rest.pop(0) for _ in range(n)] for n in (5, 5, 4, 4)]
    p = Place()
    tokens = stored.shape[0]
    blocks = tokens // 128

    barrier = pltpu.get_barrier_semaphore()
    peers = [p.along(axis, steps) for axis in range(2) for steps in range(1, SIDE)]
    peers += list(chain_peers(p, chips))
    for peer in peers:
        pl.semaphore_signal(barrier, inc=1, device_id=peer, device_id_type=MESH)

    count = lax.broadcasted_iota(jnp.int32, (R, seed.shape[1]), 0).astype(F32) + 1.0
    product = seed[...].astype(F32) * count
    levels = product - jnp.floor(product * (1.0 / 65521.0)) * 65521.0
    levels = jnp.where(levels < 0.0, levels + 65521.0, levels)
    levels = jnp.where(levels >= 65521.0, levels - 65521.0, levels)
    omega = ((levels - 32760.0) * (1.7320508 / 32760.0)).astype(BF16)
    part_s[...] = dot(hidden[...], omega, LAST)

    gains = gain[...].astype(F32)
    per_slot = acts.shape[1] // 128
    ones = jnp.ones((8, gains.shape[1]), F32)
    rows_of = [[], []]
    for block in range(blocks):
        here = pl.ds((block % per_slot) * 128, 128)
        values = acts[slots[0, block // per_slot], here, :].astype(F32)
        stored[pl.ds(block * 128, 128), :] = values
        upstream = gains * branch[block // per_slot, here, :].astype(F32)
        rows_of[0].append(dot(ones, values * values, LAST, HIGHEST)[0:1, :])
        rows_of[1].append(dot(ones, values * upstream, LAST, HIGHEST)[0:1, :])
    stat_tile[...] = jnp.concatenate(rows_of[0] + rows_of[1], 0)
    pl.semaphore_wait(barrier, len(peers))

    stats = Stats(p, stat_tile, stat_slots, stat_mid, stat_recv, stat_sent)
    first = Reduce(p, part_s, sum_s, scratch[0])
    second = Reduce(p, part_q, sum_q, scratch[1])
    square = Small(p, part_g, sum_g, scratch[2])
    cross = Small(p, part_c, sum_c, scratch[3])
    chain = Chain(p, chips, term, grad, other, above, held, chain_sems)

    stats.start()
    first.scatter_start()
    stats.middle()
    first.scatter_mid()
    total = stats.end()
    inverses = 1.0 / jnp.sqrt(total[0:blocks] / D + 1e-05)
    pulls = inverses * inverses * inverses * (total[blocks:2 * blocks] / D)
    line = lax.broadcasted_iota(jnp.int32, (blocks, gains.shape[1]), 0)
    for block in range(blocks):
        here = pl.ds(block * 128, 128)
        pick = jnp.where(line == block, 1.0, 0.0).astype(F32)
        scale = dot(inverses, pick, FIRST, HIGHEST)
        pull = dot(pulls, pick, FIRST, HIGHEST)
        values = stored[here, :]
        inside = pl.ds((block % per_slot) * 128, 128)
        upstream = gains * branch[block // per_slot, inside, :].astype(F32)
        term[here, :] = scale * upstream - values * pull
        normed[here, :] = (values * scale * gains).astype(BF16)
    chain.start()
    first.scatter_end()
    chain.slot(0)
    first.near_end()
    chain.slot(1)
    first.gather_start()
    chain.slot(2)
    first.gather_mid()
    chain.slot(3)
    first.gather_end()

    wide = normed[...]
    rows = sum(dot(wide, piece, FIRST) for piece in split(sum_s[...], 3))
    part_g[...] = dot(rows, rows, FIRST, HIGHEST)
    square.start()
    pieces = split(rows, 3)
    part_q[...] = sum(dot(wide, piece) for piece in pieces)
    second.scatter_start()
    part_c[...] = sum(dot(basis[...], piece, FIRST) for piece in pieces)
    cross.start()
    chain.slot(4)
    square.middle()
    second.scatter_mid()
    cross.middle()
    square.spread()
    second.scatter_end()
    chain.slot(5)
    square.end()
    factor_panel(0, sum_g, inverse, upper)
    second.near_end()
    cross.spread()
    factor_panel(1, sum_g, inverse, upper)
    second.gather_start()
    factor_panel(2, sum_g, inverse, upper)
    chain.slot(6)
    factor_panel(3, sum_g, inverse, upper)
    second.gather_mid()
    for panel in range(4, R // PANEL):
        factor_panel(panel, sum_g, inverse, upper)
    chain.end()
    grad_out[...] = grad[...].astype(BF16)
    cross.end()
    second.gather_end()

    mixed = 0.9 * sum(dot(piece, moment[...], FIRST) for piece in split(sum_c[...], 2))
    mixed = mixed + 0.1 * sum(dot(piece, hidden[...], FIRST) for piece in split(sum_q[...], 2))
    high, low = split(inverse[...], 2)
    mixed_high, mixed_low = split(mixed, 2)
    moment_out[...] = (dot(high, mixed_high) + dot(high, mixed_low) + dot(low, mixed_high)).astype(BF16)
    for job in (stats, first, second, square, cross, chain):
        job.finish()


def local(acts, act_slot, norm_gain, branch_grad, hidden_grad, sketch_seed, basis_old, moment_old):
    batches, rows, features = acts.shape[1:]
    tokens = batches * rows
    units = hidden_grad.shape[-1]
    chips = lax.axis_size("pipe") // 2
    vmem = pl.BlockSpec(memory_space=pltpu.VMEM)
    smem = pl.BlockSpec(memory_space=pltpu.SMEM)
    dma = pltpu.SemaphoreType.DMA
    tile = (2 * (tokens // 128), 128)
    whole = pltpu.VMEM((tokens, R), F32)
    square = pltpu.VMEM((R, R), F32)
    wide = pltpu.VMEM((tokens, features), F32)
    half = pltpu.VMEM((tokens // 2, features), F32)
    grad, moment = pl.pallas_call(
        functools.partial(kernel, chips),
        out_shape=(jax.ShapeDtypeStruct((tokens, features), BF16),
                   jax.ShapeDtypeStruct((R, units), BF16)),
        in_specs=[vmem, smem, vmem, vmem, vmem, vmem, vmem, vmem],
        out_specs=(vmem, vmem),
        scratch_shapes=[
            wide, whole, whole, pltpu.VMEM((tokens, features), BF16), wide, wide, whole, whole,
            square, square, square, square, square, square,
            pltpu.VMEM(tile, F32), pltpu.VMEM((2, SIDE - 1) + tile, F32), pltpu.VMEM(tile, F32),
            dma((2,)), dma((2,)),
            half, half, wide,
        ] + [dma((CHAIN,))] * 6
        + Reduce.scratch(tokens) + Reduce.scratch(tokens) + Small.scratch(R) + Small.scratch(R),
        compiler_params=pltpu.CompilerParams(collective_id=1, has_side_effects=True,
                                             vmem_limit_bytes=60 * 1024 * 1024),
        name="section_backward",
    )(acts[0], act_slot, norm_gain, branch_grad[0], hidden_grad[0].reshape(tokens, units),
      sketch_seed, basis_old[0], moment_old[0])
    return (grad.reshape(branch_grad.shape), moment[None])


def solution(mesh):
    in_specs = (
        P("pipe", None, None, "dp"),
        P("pipe", None),
        P("pipe", "dp"),
        P("pipe", None, None, "dp"),
        P("pipe", None, None, "dp"),
        P("pipe", "dp"),
        P("pipe", "dp", None),
        P("pipe", None, "dp"),
    )
    out_specs = (P("pipe", None, None, "dp"), P("pipe", None, "dp"))
    return jax.shard_map(local, mesh=mesh, in_specs=in_specs, out_specs=out_specs, check_vma=False)
```

```python
import functools

import jax
import jax.numpy as jnp
from jax import lax
from jax.experimental import pallas as pl
from jax.experimental.pallas import tpu as pltpu
from jax.sharding import PartitionSpec as P

D = 16384
R = 256
MESH = pl.DeviceIdType.MESH
HIGHEST = lax.Precision.HIGHEST
F32 = jnp.float32
BF16 = jnp.bfloat16
SIDE = 8
CHAIN = 4
PANEL = 64
GROUP = 8
HALVES = 2
FIRST = ((0,), (0,))
LAST = ((1,), (1,))
PLAIN = ((1,), (0,))


def dot(a, b, contract=PLAIN, precision=None):
    return lax.dot_general(a, b, (contract, ((), ())), precision=precision,
                           preferred_element_type=F32)


def split(value, count):
    parts = []
    for _ in range(count):
        part = value.astype(BF16)
        parts.append(part)
        value = value - part.astype(F32)
    return parts


class Place:
    def __init__(self):
        self.pipe = lax.axis_index("pipe")
        self.dp = lax.axis_index("dp")
        self.y, self.z = self.dp // SIDE, self.dp % SIDE
        self.core = self.pipe % 2
        self.x = self.pipe // 2
        self.turn = 1 - 2 * self.core

    def wrap(self, value):
        return (value + 2 * SIDE) % SIDE

    def along(self, axis, steps):
        if axis == 0:
            return (self.pipe, self.wrap(self.y + steps) * SIDE + self.z)
        return (self.pipe, self.y * SIDE + self.wrap(self.z + steps))

    def at(self, axis):
        return self.y if axis == 0 else self.z


def send(source, target, send_sem, recv_sem, device):
    pltpu.make_async_remote_copy(
        src_ref=source, dst_ref=target, send_sem=send_sem, recv_sem=recv_sem,
        device_id=device, device_id_type=MESH,
    ).start()


def await_bytes(like, sem):
    pltpu.make_async_copy(like, like, sem).wait()


class Reduce:
    def __init__(self, place, x, out, scratch):
        self.p, self.x, self.out = place, x, out
        self.tree, self.total, self.near, self.recv, self.sent = scratch
        self.chunk = x.shape[0] // SIDE
        self.sub = self.chunk // SIDE

    @staticmethod
    def scratch(rows):
        chunk = rows // SIDE
        return [
            pltpu.VMEM((2, 7, chunk, 128), F32),
            pltpu.VMEM((2, chunk, 128), F32),
            pltpu.VMEM((2, SIDE - 1, chunk // SIDE, 128), F32),
            pltpu.SemaphoreType.DMA((2, 8)),
            pltpu.SemaphoreType.DMA((2, 4)),
        ]

    def part(self, ref, half, index):
        rows = pl.ds(pl.multiple_of(index * self.chunk, 8), self.chunk)
        return ref.at[rows, pl.ds(128 * half, 128)]

    def owned(self, half, steps):
        p = self.p
        return p.wrap(p.at(half) + p.turn * steps)

    def tree_send(self, half, source, slot, sem, steps):
        p = self.p
        send(source, self.tree.at[half, slot], self.sent.at[half, 0], self.recv.at[half, sem],
             p.along(half, p.turn * steps))

    def scatter_start(self):
        for owner, slot, sem, steps in ((4, 0, 0, 2), (3, 1, 0, 1), (-3, 2, 1, -1),
                                        (1, 3, 2, 1), (-1, 4, 2, -1)):
            for half in range(2):
                self.tree_send(half, self.part(self.x, half, self.owned(half, owner)),
                               slot, sem, steps)

    def scatter_mid(self):
        for half in range(2):
            await_bytes(self.tree.at[half, 0:2], self.recv.at[half, 0])
            self.tree[half, 0] = (self.tree[half, 0] + self.tree[half, 1]
                                  + self.part(self.x, half, self.owned(half, 2))[...])
            self.tree_send(half, self.tree.at[half, 0], 5, 2, 2)
        for half in range(2):
            await_bytes(self.tree.at[half, 2], self.recv.at[half, 1])
            self.tree[half, 2] = (self.tree[half, 2]
                                  + self.part(self.x, half, self.owned(half, -2))[...])
            self.tree_send(half, self.tree.at[half, 2], 6, 2, -2)

    def scatter_end(self):
        p = self.p
        for half in range(2):
            await_bytes(self.tree.at[half, 3:7], self.recv.at[half, 2])
            value = self.part(self.x, half, p.at(half))[...]
            for slot in range(3, 7):
                value = value + self.tree[half, slot]
            self.total[half] = value
            for steps in (4, 3, 5, 2, 6, 1, 7):
                there = p.wrap(p.at(1 - half) + steps)
                send(self.total.at[half, pl.ds(pl.multiple_of(there * self.sub, 8), self.sub)],
                     self.near.at[half, steps - 1], self.sent.at[half, 1],
                     self.recv.at[half, 3], p.along(1 - half, steps))

    def near_end(self):
        p = self.p
        for half in range(2):
            await_bytes(self.near.at[half], self.recv.at[half, 3])
            value = self.total[half, pl.ds(pl.multiple_of(p.at(1 - half) * self.sub, 8), self.sub)]
            for slot in range(SIDE - 1):
                value = value + self.near[half, slot]
            start = p.at(half) * self.chunk + p.at(1 - half) * self.sub
            place = self.out.at[pl.ds(pl.multiple_of(start, 8), self.sub), pl.ds(128 * half, 128)]
            place[...] = value
            for steps in (4, 3, 5, 2, 6, 1, 7):
                send(place, place, self.sent.at[half, 2], self.recv.at[half, 4],
                     p.along(1 - half, steps))

    def gather_send(self, half, index, sem, steps):
        p = self.p
        place = self.part(self.out, half, index)
        send(place, place, self.sent.at[half, 3], self.recv.at[half, sem],
             p.along(half, p.turn * steps))

    def gather_start(self):
        for half in range(2):
            await_bytes(self.near.at[half], self.recv.at[half, 4])
            for sem, steps in ((5, 2), (6, -2), (7, 1), (7, -1)):
                self.gather_send(half, self.p.at(half), sem, steps)

    def gather_mid(self):
        for half in range(2):
            await_bytes(self.tree.at[half, 0], self.recv.at[half, 5])
            self.gather_send(half, self.owned(half, -2), 7, 2)
            self.gather_send(half, self.owned(half, -2), 7, 1)
        for half in range(2):
            await_bytes(self.tree.at[half, 0], self.recv.at[half, 6])
            self.gather_send(half, self.owned(half, 2), 7, -1)

    def gather_end(self):
        for half in range(2):
            await_bytes(self.tree.at[half, 0:5], self.recv.at[half, 7])

    def finish(self):
        for half in range(2):
            await_bytes(self.tree.at[half], self.sent.at[half, 0])
            await_bytes(self.near.at[half], self.sent.at[half, 1])
            await_bytes(self.near.at[half], self.sent.at[half, 2])
            await_bytes(self.tree.at[half], self.sent.at[half, 3])


class Small:
    def __init__(self, place, x, out, scratch):
        self.p, self.x, self.out = place, x, out
        self.slots, self.mid, self.recv, self.sent = scratch
        self.chunk = x.shape[0] // SIDE

    @staticmethod
    def scratch(rows):
        chunk = rows // SIDE
        return [
            pltpu.VMEM((2, 2, SIDE - 1, chunk, 128), F32),
            pltpu.VMEM((2, chunk, 128), F32),
            pltpu.SemaphoreType.DMA((2, 3)),
            pltpu.SemaphoreType.DMA((2, 3)),
        ]

    def part(self, ref, half, index):
        rows = pl.ds(pl.multiple_of(index * self.chunk, 8), self.chunk)
        return ref.at[rows, pl.ds(128 * half, 128)]

    def start(self):
        p = self.p
        for steps in (4, 3, 5, 2, 6, 1, 7):
            for half in range(2):
                send(self.part(self.x, half, p.wrap(p.at(half) + steps)),
                     self.slots.at[0, half, steps - 1], self.sent.at[half, 0],
                     self.recv.at[half, 0], p.along(half, steps))

    def total(self, stage, half, value):
        await_bytes(self.slots.at[stage, half], self.recv.at[half, stage])
        for slot in range(SIDE - 1):
            value = value + self.slots[stage, half, slot]
        return value

    def middle(self):
        p = self.p
        for half in range(2):
            self.mid[half] = self.total(0, half, self.part(self.x, half, p.at(half))[...])
            for steps in (4, 3, 5, 2, 6, 1, 7):
                send(self.mid.at[half], self.slots.at[1, half, steps - 1], self.sent.at[half, 1],
                     self.recv.at[half, 1], p.along(1 - half, steps))

    def spread(self):
        p = self.p
        for half in range(2):
            place = self.part(self.out, half, p.at(half))
            place[...] = self.total(1, half, self.mid[half])
            for steps in (4, 3, 5, 2, 6, 1, 7):
                send(place, place, self.sent.at[half, 2], self.recv.at[half, 2],
                     p.along(half, steps))

    def end(self):
        for half in range(2):
            await_bytes(self.slots.at[0, half], self.recv.at[half, 2])

    def finish(self):
        for half in range(2):
            for stage in range(3):
                await_bytes(self.slots.at[0, half], self.sent.at[half, stage])


class Stats:
    def __init__(self, place, tile, slots, mid, recv, sent):
        self.p, self.tile, self.slots, self.mid = place, tile, slots, mid
        self.recv, self.sent = recv, sent

    def push(self, source, axis):
        for steps in (4, 3, 5, 2, 6, 1, 7):
            send(source, self.slots.at[axis, steps - 1], self.sent.at[axis], self.recv.at[axis],
                 self.p.along(axis, steps))

    def total(self, source, axis):
        await_bytes(self.slots.at[axis], self.recv.at[axis])
        value = source[...]
        for slot in range(SIDE - 1):
            value = value + self.slots[axis, slot]
        return value

    def start(self):
        self.push(self.tile, 0)

    def middle(self):
        self.mid[...] = self.total(self.tile, 0)
        self.push(self.mid, 1)

    def end(self):
        return self.total(self.mid, 1)

    def finish(self):
        for axis in range(2):
            await_bytes(self.slots.at[axis], self.sent.at[axis])


class Chain:
    def __init__(self, place, chips, term, grad, other, above, held, sems):
        self.p, self.chips = place, chips
        self.term, self.grad, self.other, self.above, self.held = term, grad, other, above, held
        self.pair_s, self.pair_r, self.down_s, self.down_r, self.give_s, self.give_r = sems
        self.half_rows = term.shape[0] // 2
        self.size = self.half_rows // CHAIN
        self.partner, self.upper, self.lower = chain_peers(place, chips)

    def rows(self, core, index):
        return pl.ds(pl.multiple_of(core * self.half_rows + index * self.size, 8), self.size)

    def remote(self, source, target, send_sem, recv_sem, device):
        return pltpu.make_async_remote_copy(
            src_ref=source, dst_ref=target, send_sem=send_sem, recv_sem=recv_sem,
            device_id=device, device_id_type=MESH)

    def pair(self, index):
        here = pl.ds(index * self.size, self.size)
        return self.remote(self.term.at[self.rows(1 - self.p.core, index)], self.other.at[here],
                           self.pair_s.at[index], self.pair_r.at[index], self.partner)

    def down(self, index):
        here = pl.ds(index * self.size, self.size)
        return self.remote(self.held.at[here], self.above.at[here],
                           self.down_s.at[index], self.down_r.at[index], self.lower)

    def give(self, index):
        here = pl.ds(self.half_rows + index * self.size, self.size)
        return self.remote(self.held.at[here], self.grad.at[self.rows(self.p.core, index)],
                           self.give_s.at[index], self.give_r.at[index], self.partner)

    def start(self):
        for index in range(CHAIN):
            self.pair(index).start()

    def slot(self, slot):
        for shift in range(self.chips):
            index = slot - shift
            if 0 <= index < CHAIN:
                @pl.when(self.p.x == self.chips - 1 - shift)
                def _():
                    here = pl.ds(index * self.size, self.size)
                    self.pair(index).wait_recv()
                    own_sum = self.term[self.rows(self.p.core, index)]
                    mate = self.other[here]
                    mate_sum = mate
                    if shift > 0:
                        self.down(index).wait_recv()
                        own_sum = own_sum + self.above[here]
                        mate_sum = mate + self.above[here]
                    both = own_sum + mate
                    lead = self.p.core == 0
                    self.held[here] = both
                    self.held[pl.ds(self.half_rows + index * self.size, self.size)] = jnp.where(
                        lead, mate_sum, both)
                    self.grad[self.rows(self.p.core, index)] = jnp.where(lead, both, own_sum)
                    if shift < self.chips - 1:
                        self.down(index).start()
                    self.give(index).start()

    def end(self):
        for index in range(CHAIN):
            place = self.grad.at[self.rows(1 - self.p.core, index)]
            await_bytes(place, self.give_r.at[index])

    def finish(self):
        for index in range(CHAIN):
            self.pair(index).wait_send()
            self.give(index).wait_send()

        @pl.when(self.p.x > 0)
        def _():
            for index in range(CHAIN):
                self.down(index).wait_send()


def chain_peers(p, chips):
    return ((p.x * 2 + 1 - p.core, p.dp),
            (((p.x + 1) % chips) * 2 + p.core, p.dp),
            (((p.x + chips - 1) % chips) * 2 + p.core, p.dp))


def eliminate(value, width, row):
    for k in range(0, width, GROUP):
        columns = [jnp.broadcast_to(value[:, k + j:k + j + 1], value.shape) for j in range(GROUP)]
        scales, low, uppers, weights = [], {}, [], []
        for j in range(GROUP):
            pivot = columns[j][k + j:k + j + 1, :]
            for m in range(j):
                pivot = pivot - low[j, m] * low[j, m]
            scales.append(lax.rsqrt(pivot))
            for i in range(j + 1, GROUP):
                entry = columns[j][k + i:k + i + 1, :]
                for m in range(j):
                    entry = entry - low[i, m] * low[j, m]
                low[i, j] = entry * scales[j]
        for j in range(GROUP):
            upper, weight = value[k + j:k + j + 1, :], columns[j]
            for m in range(j):
                upper = upper - low[j, m] * uppers[m]
                weight = weight - weights[m] * low[j, m]
            uppers.append(upper * scales[j])
            weights.append(weight * scales[j])
        updated = value
        for j in range(GROUP):
            updated = updated - weights[j] * uppers[j]
        for j in range(GROUP):
            updated = jnp.where(row == k + j, uppers[j], updated)
        value = jnp.where(row < k, value, updated)
    return value


def factor_panel(panel, gram, inverse, upper):
    width = PANEL
    start = panel * width
    here = pl.ds(start, width)
    row = lax.broadcasted_iota(jnp.int32, (width, 128), 0)
    lane = lax.broadcasted_iota(jnp.int32, (width, 128), 1)
    block = gram[here, :]
    wide = lax.broadcasted_iota(jnp.int32, (width, R), 1)
    deep = lax.broadcasted_iota(jnp.int32, (width, R), 0)
    target = jnp.where(wide == deep + start, 1.0, 0.0).astype(F32)
    if panel > 0:
        before = upper[0:start, :]
        left = before[:, start:start + width]
        block = block - dot(left, before, FIRST, HIGHEST)
        target = target - dot(left, inverse[0:start, :], FIRST, HIGHEST)
    tile = block[:, 128 * (start // 128):128 * (start // 128) + 128]
    shift = start % 128
    if shift:
        tile = pltpu.roll(tile, 128 - shift, 1)
    value = jnp.where(lane < width, tile, jnp.where(lane == row + width, 1.0, 0.0).astype(F32))
    value = eliminate(value, width, row)
    corner = value[:, width:2 * width]
    upper[here, :] = dot(corner, block, PLAIN, HIGHEST)
    inverse[here, :] = dot(corner, target, PLAIN, HIGHEST)


def kernel(chips, acts, slots, gain, branch, hidden, seed, basis, moment, grad_out, moment_out,
           stored, part_s, sum_s, normed, term, grad, part_q, sum_q, part_g, sum_g, part_c, sum_c,
           inverse, upper, stat_tile, stat_slots, stat_mid, stat_recv, stat_sent,
           other, above, held, *rest):
    rest = list(rest)
    chain_sems = [rest.pop(0) for _ in range(6)]
    firsts = [[rest.pop(0) for _ in range(5)] for _ in range(HALVES)]
    seconds = [[rest.pop(0) for _ in range(5)] for _ in range(HALVES)]
    scratch = [[rest.pop(0) for _ in range(4)] for _ in range(2)]
    p = Place()
    tokens = stored.shape[0]
    blocks = tokens // 128

    barrier = pltpu.get_barrier_semaphore()
    peers = [p.along(axis, steps) for axis in range(2) for steps in range(1, SIDE)]
    peers += list(chain_peers(p, chips))
    for peer in peers:
        pl.semaphore_signal(barrier, inc=1, device_id=peer, device_id_type=MESH)

    count = lax.broadcasted_iota(jnp.int32, (R, seed.shape[1]), 0).astype(F32) + 1.0
    product = seed[...].astype(F32) * count
    levels = product - jnp.floor(product * (1.0 / 65521.0)) * 65521.0
    levels = jnp.where(levels < 0.0, levels + 65521.0, levels)
    levels = jnp.where(levels >= 65521.0, levels - 65521.0, levels)
    omega = ((levels - 32760.0) * (1.7320508 / 32760.0)).astype(BF16)
    for batch in range(hidden.shape[0]):
        part_s[pl.ds(batch * R, R), :] = dot(omega, hidden[batch])

    gains = gain[...].astype(F32)
    per_slot = acts.shape[1] // 128
    ones = jnp.ones((8, gains.shape[1]), F32)
    rows_of = [[], []]
    for block in range(blocks):
        here = pl.ds((block % per_slot) * 128, 128)
        values = acts[slots[0, block // per_slot], here, :].astype(F32)
        stored[pl.ds(block * 128, 128), :] = values
        upstream = gains * branch[block // per_slot, here, :].astype(F32)
        rows_of[0].append(dot(ones, values * values, LAST, HIGHEST)[0:1, :])
        rows_of[1].append(dot(ones, values * upstream, LAST, HIGHEST)[0:1, :])
    stat_tile[...] = jnp.concatenate(rows_of[0] + rows_of[1], 0)
    pl.semaphore_wait(barrier, len(peers))

    stats = Stats(p, stat_tile, stat_slots, stat_mid, stat_recv, stat_sent)
    share = tokens // HALVES
    spans = [pl.ds(index * share, share) for index in range(HALVES)]
    first = [Reduce(p, part_s.at[span], sum_s.at[span], own) for span, own in zip(spans, firsts)]
    second = [Reduce(p, part_q.at[span], sum_q.at[span], own) for span, own in zip(spans, seconds)]
    square = Small(p, part_g, sum_g, scratch[0])
    cross = Small(p, part_c, sum_c, scratch[1])
    chain = Chain(p, chips, term, grad, other, above, held, chain_sems)
    per_part = hidden.shape[0] // HALVES

    def every(jobs, step):
        for job in jobs:
            getattr(job, step)()

    every(first, "scatter_start")
    stats.start()
    every(first, "scatter_mid")
    stats.middle()
    every(first, "scatter_end")
    total = stats.end()
    inverses = 1.0 / jnp.sqrt(total[0:blocks] / D + 1e-05)
    pulls = inverses * inverses * inverses * (total[blocks:2 * blocks] / D)
    line = lax.broadcasted_iota(jnp.int32, (blocks, gains.shape[1]), 0)
    for block in range(blocks):
        here = pl.ds(block * 128, 128)
        pick = jnp.where(line == block, 1.0, 0.0).astype(F32)
        scale = dot(inverses, pick, FIRST, HIGHEST)
        pull = dot(pulls, pick, FIRST, HIGHEST)
        values = stored[here, :]
        inside = pl.ds((block % per_slot) * 128, 128)
        upstream = gains * branch[block // per_slot, inside, :].astype(F32)
        term[here, :] = scale * upstream - values * pull
        normed[here, :] = (values * scale * gains).astype(BF16)
    every(first, "near_end")
    chain.start()
    every(first, "gather_start")
    chain.slot(0)
    every(first, "gather_mid")
    chain.slot(1)

    rows = jnp.zeros((R, gains.shape[1]), F32)
    for index in range(HALVES):
        first[index].gather_end()
        for batch in range(index * per_part, (index + 1) * per_part):
            wide = normed[pl.ds(batch * acts.shape[1], acts.shape[1]), :]
            for piece in split(sum_s[pl.ds(batch * R, R), :], 3):
                rows = rows + dot(piece, wide)
    pieces = split(rows, 3)
    for index in range(HALVES):
        part_q[spans[index], :] = sum(dot(normed[spans[index], :], piece, LAST) for piece in pieces)
        second[index].scatter_start()
    part_g[...] = dot(rows, rows, LAST, HIGHEST)
    square.start()
    chain.slot(2)
    part_c[...] = sum(dot(piece, basis[...]) for piece in pieces)
    every(second, "scatter_mid")
    square.middle()
    cross.start()
    chain.slot(3)
    every(second, "scatter_end")
    square.spread()
    chain.slot(4)
    every(second, "near_end")
    cross.middle()
    square.end()
    factor_panel(0, sum_g, inverse, upper)
    every(second, "gather_start")
    cross.spread()
    factor_panel(1, sum_g, inverse, upper)
    chain.slot(5)
    factor_panel(2, sum_g, inverse, upper)
    every(second, "gather_mid")
    factor_panel(3, sum_g, inverse, upper)
    chain.slot(6)
    chain.end()
    grad_out[...] = grad[...]
    cross.end()

    mixed = 0.9 * sum(dot(moment[...], piece, LAST) for piece in split(sum_c[...], 2))
    high, low = split(inverse[...], 2)
    for index in range(HALVES):
        second[index].gather_end()
        for batch in range(index * per_part, (index + 1) * per_part):
            for piece in split(sum_q[pl.ds(batch * acts.shape[1], acts.shape[1]), :], 2):
                mixed = mixed + 0.1 * dot(hidden[batch], piece)
    mixed_high, mixed_low = split(mixed, 2)
    moment_out[...] = (dot(mixed_high, high, LAST) + dot(mixed_low, high, LAST)
                       + dot(mixed_high, low, LAST))
    for job in (stats, *first, *second, square, cross, chain):
        job.finish()


def local(acts, act_slot, norm_gain, branch_grad, hidden_grad, sketch_seed, basis_old, moment_old):
    batches, rows, features = acts.shape[1:]
    tokens = batches * rows
    units = hidden_grad.shape[-1]
    chips = lax.axis_size("pipe") // 2
    vmem = pl.BlockSpec(memory_space=pltpu.VMEM)
    smem = pl.BlockSpec(memory_space=pltpu.SMEM)
    dma = pltpu.SemaphoreType.DMA
    tile = (2 * (tokens // 128), 128)
    whole = pltpu.VMEM((tokens, R), F32)
    square = pltpu.VMEM((R, R), F32)
    wide = pltpu.VMEM((tokens, features), F32)
    half = pltpu.VMEM((tokens // 2, features), F32)
    grad, moment = pl.pallas_call(
        functools.partial(kernel, chips),
        out_shape=(jax.ShapeDtypeStruct((tokens, features), F32),
                   jax.ShapeDtypeStruct((units, R), F32)),
        in_specs=[vmem, smem, vmem, vmem, vmem, vmem, vmem, vmem],
        out_specs=(vmem, vmem),
        scratch_shapes=[
            wide, whole, whole, pltpu.VMEM((tokens, features), BF16), wide, wide, whole, whole,
            square, square, square, square, square, square,
            pltpu.VMEM(tile, F32), pltpu.VMEM((2, SIDE - 1) + tile, F32), pltpu.VMEM(tile, F32),
            dma((2,)), dma((2,)),
            half, half, wide,
        ] + [dma((CHAIN,))] * 6
        + Reduce.scratch(tokens // HALVES) * (2 * HALVES) + Small.scratch(R) * 2,
        compiler_params=pltpu.CompilerParams(collective_id=1, has_side_effects=True,
                                             vmem_limit_bytes=60 * 1024 * 1024),
        name="section_backward",
    )(acts[0], act_slot, norm_gain, branch_grad[0], hidden_grad[0].swapaxes(1, 2),
      sketch_seed, basis_old[0], moment_old[0].T)
    return (grad.astype(BF16).reshape(branch_grad.shape), moment.astype(BF16).T[None])


def solution(mesh):
    in_specs = (
        P("pipe", None, None, "dp"),
        P("pipe", None),
        P("pipe", "dp"),
        P("pipe", None, None, "dp"),
        P("pipe", None, None, "dp"),
        P("pipe", "dp"),
        P("pipe", "dp", None),
        P("pipe", None, "dp"),
    )
    out_specs = (P("pipe", None, None, "dp"), P("pipe", None, "dp"))
    return jax.shard_map(local, mesh=mesh, in_specs=in_specs, out_specs=out_specs, check_vma=False)
```

```python
import functools

import jax
import jax.numpy as jnp
from jax import lax
from jax.experimental import pallas as pl
from jax.experimental.pallas import tpu as pltpu
from jax.sharding import PartitionSpec as P

D = 16384
R = 256
MESH = pl.DeviceIdType.MESH
HIGHEST = lax.Precision.HIGHEST
F32 = jnp.float32
BF16 = jnp.bfloat16
SIDE = 8
CHAIN = 4
PANEL = 64
GROUP = 8
HALVES = 2
FIRST = ((0,), (0,))
LAST = ((1,), (1,))
PLAIN = ((1,), (0,))


def dot(a, b, contract=PLAIN, precision=None):
    return lax.dot_general(a, b, (contract, ((), ())), precision=precision,
                           preferred_element_type=F32)


def split(value, count):
    parts = []
    for _ in range(count):
        part = value.astype(BF16)
        parts.append(part)
        value = value - part.astype(F32)
    return parts


def row_sums(values):
    ones = jnp.ones((8, values.shape[1]), BF16)
    return sum(dot(ones, piece, LAST) for piece in split(values, 3))[0:1, :]


class Place:
    def __init__(self):
        self.pipe = lax.axis_index("pipe")
        self.dp = lax.axis_index("dp")
        self.y, self.z = self.dp // SIDE, self.dp % SIDE
        self.core = self.pipe % 2
        self.x = self.pipe // 2
        self.turn = 1 - 2 * self.core

    def wrap(self, value):
        return (value + 2 * SIDE) % SIDE

    def along(self, axis, steps):
        if axis == 0:
            return (self.pipe, self.wrap(self.y + steps) * SIDE + self.z)
        return (self.pipe, self.y * SIDE + self.wrap(self.z + steps))

    def at(self, axis):
        return self.y if axis == 0 else self.z


def send(source, target, send_sem, recv_sem, device):
    pltpu.make_async_remote_copy(
        src_ref=source, dst_ref=target, send_sem=send_sem, recv_sem=recv_sem,
        device_id=device, device_id_type=MESH,
    ).start()


def await_bytes(like, sem):
    pltpu.make_async_copy(like, like, sem).wait()


class Reduce:
    def __init__(self, place, x, out, scratch):
        self.p, self.x, self.out = place, x, out
        self.tree, self.total, self.near, self.recv, self.sent = scratch
        self.chunk = x.shape[0] // SIDE
        self.sub = self.chunk // SIDE

    @staticmethod
    def scratch(rows):
        chunk = rows // SIDE
        return [
            pltpu.VMEM((2, 7, chunk, 128), F32),
            pltpu.VMEM((2, chunk, 128), F32),
            pltpu.VMEM((2, SIDE - 1, chunk // SIDE, 128), F32),
            pltpu.SemaphoreType.DMA((2, 8)),
            pltpu.SemaphoreType.DMA((2, 4)),
        ]

    def part(self, ref, half, index):
        rows = pl.ds(pl.multiple_of(index * self.chunk, 8), self.chunk)
        return ref.at[rows, pl.ds(128 * half, 128)]

    def owned(self, half, steps):
        p = self.p
        return p.wrap(p.at(half) + p.turn * steps)

    def tree_send(self, half, source, slot, sem, steps):
        p = self.p
        send(source, self.tree.at[half, slot], self.sent.at[half, 0], self.recv.at[half, sem],
             p.along(half, p.turn * steps))

    def scatter_start(self):
        for owner, slot, sem, steps in ((4, 0, 0, 2), (3, 1, 0, 1), (-3, 2, 1, -1),
                                        (1, 3, 2, 1), (-1, 4, 2, -1)):
            for half in range(2):
                self.tree_send(half, self.part(self.x, half, self.owned(half, owner)),
                               slot, sem, steps)

    def scatter_mid(self):
        for half in range(2):
            await_bytes(self.tree.at[half, 0:2], self.recv.at[half, 0])
            self.tree[half, 0] = (self.tree[half, 0] + self.tree[half, 1]
                                  + self.part(self.x, half, self.owned(half, 2))[...])
            self.tree_send(half, self.tree.at[half, 0], 5, 2, 2)
        for half in range(2):
            await_bytes(self.tree.at[half, 2], self.recv.at[half, 1])
            self.tree[half, 2] = (self.tree[half, 2]
                                  + self.part(self.x, half, self.owned(half, -2))[...])
            self.tree_send(half, self.tree.at[half, 2], 6, 2, -2)

    def scatter_end(self):
        p = self.p
        for half in range(2):
            await_bytes(self.tree.at[half, 3:7], self.recv.at[half, 2])
            value = self.part(self.x, half, p.at(half))[...]
            for slot in range(3, 7):
                value = value + self.tree[half, slot]
            self.total[half] = value
            for steps in (4, 3, 5, 2, 6, 1, 7):
                there = p.wrap(p.at(1 - half) + steps)
                send(self.total.at[half, pl.ds(pl.multiple_of(there * self.sub, 8), self.sub)],
                     self.near.at[half, steps - 1], self.sent.at[half, 1],
                     self.recv.at[half, 3], p.along(1 - half, steps))

    def near_end(self):
        p = self.p
        for half in range(2):
            await_bytes(self.near.at[half], self.recv.at[half, 3])
            value = self.total[half, pl.ds(pl.multiple_of(p.at(1 - half) * self.sub, 8), self.sub)]
            for slot in range(SIDE - 1):
                value = value + self.near[half, slot]
            start = p.at(half) * self.chunk + p.at(1 - half) * self.sub
            place = self.out.at[pl.ds(pl.multiple_of(start, 8), self.sub), pl.ds(128 * half, 128)]
            place[...] = value
            for steps in (4, 3, 5, 2, 6, 1, 7):
                send(place, place, self.sent.at[half, 2], self.recv.at[half, 4],
                     p.along(1 - half, steps))

    def gather_send(self, half, index, sem, steps):
        p = self.p
        place = self.part(self.out, half, index)
        send(place, place, self.sent.at[half, 3], self.recv.at[half, sem],
             p.along(half, p.turn * steps))

    def gather_start(self):
        for half in range(2):
            await_bytes(self.near.at[half], self.recv.at[half, 4])
            for sem, steps in ((5, 2), (6, -2), (7, 1), (7, -1)):
                self.gather_send(half, self.p.at(half), sem, steps)

    def gather_mid(self):
        for half in range(2):
            await_bytes(self.tree.at[half, 0], self.recv.at[half, 5])
            self.gather_send(half, self.owned(half, -2), 7, 2)
            self.gather_send(half, self.owned(half, -2), 7, 1)
        for half in range(2):
            await_bytes(self.tree.at[half, 0], self.recv.at[half, 6])
            self.gather_send(half, self.owned(half, 2), 7, -1)

    def gather_end(self):
        for half in range(2):
            await_bytes(self.tree.at[half, 0:5], self.recv.at[half, 7])

    def finish(self):
        for half in range(2):
            await_bytes(self.tree.at[half], self.sent.at[half, 0])
            await_bytes(self.near.at[half], self.sent.at[half, 1])
            await_bytes(self.near.at[half], self.sent.at[half, 2])
            await_bytes(self.tree.at[half], self.sent.at[half, 3])


class Small:
    def __init__(self, place, x, out, scratch):
        self.p, self.x, self.out = place, x, out
        self.slots, self.mid, self.recv, self.sent = scratch
        self.chunk = x.shape[0] // SIDE

    @staticmethod
    def scratch(rows):
        chunk = rows // SIDE
        return [
            pltpu.VMEM((2, 2, SIDE - 1, chunk, 128), F32),
            pltpu.VMEM((2, chunk, 128), F32),
            pltpu.SemaphoreType.DMA((2, 3)),
            pltpu.SemaphoreType.DMA((2, 3)),
        ]

    def part(self, ref, half, index):
        rows = pl.ds(pl.multiple_of(index * self.chunk, 8), self.chunk)
        return ref.at[rows, pl.ds(128 * half, 128)]

    def start(self):
        p = self.p
        for steps in (4, 3, 5, 2, 6, 1, 7):
            for half in range(2):
                send(self.part(self.x, half, p.wrap(p.at(half) + steps)),
                     self.slots.at[0, half, steps - 1], self.sent.at[half, 0],
                     self.recv.at[half, 0], p.along(half, steps))

    def total(self, stage, half, value):
        await_bytes(self.slots.at[stage, half], self.recv.at[half, stage])
        for slot in range(SIDE - 1):
            value = value + self.slots[stage, half, slot]
        return value

    def middle(self):
        p = self.p
        for half in range(2):
            self.mid[half] = self.total(0, half, self.part(self.x, half, p.at(half))[...])
            for steps in (4, 3, 5, 2, 6, 1, 7):
                send(self.mid.at[half], self.slots.at[1, half, steps - 1], self.sent.at[half, 1],
                     self.recv.at[half, 1], p.along(1 - half, steps))

    def spread(self):
        p = self.p
        for half in range(2):
            place = self.part(self.out, half, p.at(half))
            place[...] = self.total(1, half, self.mid[half])
            for steps in (4, 3, 5, 2, 6, 1, 7):
                send(place, place, self.sent.at[half, 2], self.recv.at[half, 2],
                     p.along(half, steps))

    def end(self):
        for half in range(2):
            await_bytes(self.slots.at[0, half], self.recv.at[half, 2])

    def finish(self):
        for half in range(2):
            for stage in range(3):
                await_bytes(self.slots.at[0, half], self.sent.at[half, stage])


class Stats:
    def __init__(self, place, tile, slots, mid, recv, sent):
        self.p, self.tile, self.slots, self.mid = place, tile, slots, mid
        self.recv, self.sent = recv, sent

    def push(self, source, axis):
        for steps in (4, 3, 5, 2, 6, 1, 7):
            send(source, self.slots.at[axis, steps - 1], self.sent.at[axis], self.recv.at[axis],
                 self.p.along(axis, steps))

    def total(self, source, axis):
        await_bytes(self.slots.at[axis], self.recv.at[axis])
        value = source[...]
        for slot in range(SIDE - 1):
            value = value + self.slots[axis, slot]
        return value

    def start(self):
        self.push(self.tile, 0)

    def middle(self):
        self.mid[...] = self.total(self.tile, 0)
        self.push(self.mid, 1)

    def end(self):
        return self.total(self.mid, 1)

    def finish(self):
        for axis in range(2):
            await_bytes(self.slots.at[axis], self.sent.at[axis])


class Chain:
    def __init__(self, place, chips, term, grad, other, above, held, sems):
        self.p, self.chips = place, chips
        self.term, self.grad, self.other, self.above, self.held = term, grad, other, above, held
        self.pair_s, self.pair_r, self.down_s, self.down_r, self.give_s, self.give_r = sems
        self.half_rows = term.shape[0] // 2
        self.size = self.half_rows // CHAIN
        self.partner, self.upper, self.lower = chain_peers(place, chips)

    def rows(self, core, index):
        return pl.ds(pl.multiple_of(core * self.half_rows + index * self.size, 8), self.size)

    def remote(self, source, target, send_sem, recv_sem, device):
        return pltpu.make_async_remote_copy(
            src_ref=source, dst_ref=target, send_sem=send_sem, recv_sem=recv_sem,
            device_id=device, device_id_type=MESH)

    def pair(self, index):
        here = pl.ds(index * self.size, self.size)
        return self.remote(self.term.at[self.rows(1 - self.p.core, index)], self.other.at[here],
                           self.pair_s.at[index], self.pair_r.at[index], self.partner)

    def down(self, index):
        here = pl.ds(index * self.size, self.size)
        return self.remote(self.held.at[here], self.above.at[here],
                           self.down_s.at[index], self.down_r.at[index], self.lower)

    def give(self, index):
        here = pl.ds(self.half_rows + index * self.size, self.size)
        return self.remote(self.held.at[here], self.grad.at[self.rows(self.p.core, index)],
                           self.give_s.at[index], self.give_r.at[index], self.partner)

    def start(self):
        for index in range(CHAIN):
            self.pair(index).start()

    def slot(self, slot):
        for shift in range(self.chips):
            index = slot - shift
            if 0 <= index < CHAIN:
                @pl.when(self.p.x == self.chips - 1 - shift)
                def _():
                    here = pl.ds(index * self.size, self.size)
                    self.pair(index).wait_recv()
                    own_sum = self.term[self.rows(self.p.core, index)]
                    mate = self.other[here]
                    mate_sum = mate
                    if shift > 0:
                        self.down(index).wait_recv()
                        own_sum = own_sum + self.above[here]
                        mate_sum = mate + self.above[here]
                    both = own_sum + mate
                    lead = self.p.core == 0
                    self.held[here] = both
                    self.held[pl.ds(self.half_rows + index * self.size, self.size)] = jnp.where(
                        lead, mate_sum, both)
                    self.grad[self.rows(self.p.core, index)] = jnp.where(lead, both, own_sum)
                    if shift < self.chips - 1:
                        self.down(index).start()
                    self.give(index).start()

    def end(self):
        for index in range(CHAIN):
            place = self.grad.at[self.rows(1 - self.p.core, index)]
            await_bytes(place, self.give_r.at[index])

    def finish(self):
        for index in range(CHAIN):
            self.pair(index).wait_send()
            self.give(index).wait_send()

        @pl.when(self.p.x > 0)
        def _():
            for index in range(CHAIN):
                self.down(index).wait_send()


def chain_peers(p, chips):
    return ((p.x * 2 + 1 - p.core, p.dp),
            (((p.x + 1) % chips) * 2 + p.core, p.dp),
            (((p.x + chips - 1) % chips) * 2 + p.core, p.dp))


def eliminate(value, width, row):
    for k in range(0, width, GROUP):
        columns = [jnp.broadcast_to(value[:, k + j:k + j + 1], value.shape) for j in range(GROUP)]
        scales, low, uppers, weights = [], {}, [], []
        for j in range(GROUP):
            pivot = columns[j][k + j:k + j + 1, :]
            for m in range(j):
                pivot = pivot - low[j, m] * low[j, m]
            scales.append(lax.rsqrt(pivot))
            for i in range(j + 1, GROUP):
                entry = columns[j][k + i:k + i + 1, :]
                for m in range(j):
                    entry = entry - low[i, m] * low[j, m]
                low[i, j] = entry * scales[j]
        for j in range(GROUP):
            upper, weight = value[k + j:k + j + 1, :], columns[j]
            for m in range(j):
                upper = upper - low[j, m] * uppers[m]
                weight = weight - weights[m] * low[j, m]
            uppers.append(upper * scales[j])
            weights.append(weight * scales[j])
        updated = value
        for j in range(GROUP):
            updated = updated - weights[j] * uppers[j]
        for j in range(GROUP):
            updated = jnp.where(row == k + j, uppers[j], updated)
        value = jnp.where(row < k, value, updated)
    return value


def gram_rows(panel, gram):
    if panel < 2:
        right = gram[128:192, 128 * panel:128 * panel + 128]
        return jnp.concatenate([gram[PANEL * panel:PANEL * (panel + 1), 0:128], right], 1)
    right = gram[PANEL * (panel - 2):PANEL * (panel - 1), 128:256]
    return jnp.concatenate([jnp.zeros((PANEL, 128), F32), right], 1)


def factor_panel(panel, gram, inverse, upper):
    width = PANEL
    start = panel * width
    here = pl.ds(start, width)
    row = lax.broadcasted_iota(jnp.int32, (width, 128), 0)
    lane = lax.broadcasted_iota(jnp.int32, (width, 128), 1)
    block = gram_rows(panel, gram)
    wide = lax.broadcasted_iota(jnp.int32, (width, R), 1)
    deep = lax.broadcasted_iota(jnp.int32, (width, R), 0)
    target = jnp.where(wide == deep + start, 1.0, 0.0).astype(F32)
    if panel > 0:
        before = upper[0:start, :]
        left = before[:, start:start + width]
        block = block - dot(left, before, FIRST, HIGHEST)
        target = target - dot(left, inverse[0:start, :], FIRST, HIGHEST)
    tile = block[:, 128 * (start // 128):128 * (start // 128) + 128]
    shift = start % 128
    if shift:
        tile = pltpu.roll(tile, 128 - shift, 1)
    value = jnp.where(lane < width, tile, jnp.where(lane == row + width, 1.0, 0.0).astype(F32))
    value = eliminate(value, width, row)
    corner = value[:, width:2 * width]
    upper[here, :] = dot(corner, block, PLAIN, HIGHEST)
    inverse[here, :] = dot(corner, target, PLAIN, HIGHEST)


def kernel(chips, acts, slots, gain, branch, hidden, seed, basis, moment, grad_out, moment_out,
           stored, part_s, sum_s, normed, term, grad, part_q, sum_q, part_g, sum_g, part_c, sum_c,
           inverse, upper, stat_tile, stat_slots, stat_mid, stat_recv, stat_sent,
           other, above, held, *rest):
    rest = list(rest)
    chain_sems = [rest.pop(0) for _ in range(6)]
    firsts = [[rest.pop(0) for _ in range(5)] for _ in range(HALVES)]
    seconds = [[rest.pop(0) for _ in range(5)] for _ in range(HALVES)]
    scratch = [[rest.pop(0) for _ in range(4)] for _ in range(2)]
    p = Place()
    tokens = stored.shape[0]
    blocks = tokens // 128
    per_part = hidden.shape[0] // HALVES

    barrier = pltpu.get_barrier_semaphore()
    peers = [p.along(axis, steps) for axis in range(2) for steps in range(1, SIDE)]
    peers += list(chain_peers(p, chips))
    for peer in peers:
        pl.semaphore_signal(barrier, inc=1, device_id=peer, device_id_type=MESH)

    count = lax.broadcasted_iota(jnp.int32, (R, seed.shape[1]), 0).astype(F32) + 1.0
    product = seed[...].astype(F32) * count
    levels = product - jnp.floor(product * (1.0 / 65521.0)) * 65521.0
    levels = jnp.where(levels < 0.0, levels + 65521.0, levels)
    levels = jnp.where(levels >= 65521.0, levels - 65521.0, levels)
    omega = ((levels - 32760.0) * (1.7320508 / 32760.0)).astype(BF16)

    def sketch_share(index):
        for batch in range(index * per_part, (index + 1) * per_part):
            part_s[pl.ds(batch * R, R), :] = dot(omega, hidden[batch])

    sketch_share(0)
    pl.semaphore_wait(barrier, len(peers))

    stats = Stats(p, stat_tile, stat_slots, stat_mid, stat_recv, stat_sent)
    share = tokens // HALVES
    spans = [pl.ds(index * share, share) for index in range(HALVES)]
    first = [Reduce(p, part_s.at[span], sum_s.at[span], own) for span, own in zip(spans, firsts)]
    second = [Reduce(p, part_q.at[span], sum_q.at[span], own) for span, own in zip(spans, seconds)]
    square = Small(p, part_g, sum_g, scratch[0])
    cross = Small(p, part_c, sum_c, scratch[1])
    chain = Chain(p, chips, term, grad, other, above, held, chain_sems)

    def every(jobs, step):
        for job in jobs:
            getattr(job, step)()

    first[0].scatter_start()
    for index in range(1, HALVES):
        sketch_share(index)
        first[index].scatter_start()
    gains = gain[...].astype(F32)
    per_slot = acts.shape[1] // 128
    rows_of = [[], []]
    for block in range(blocks):
        here = pl.ds((block % per_slot) * 128, 128)
        values = acts[slots[0, block // per_slot], here, :].astype(F32)
        stored[pl.ds(block * 128, 128), :] = values
        upstream = gains * branch[block // per_slot, here, :].astype(F32)
        rows_of[0].append(row_sums(values * values))
        rows_of[1].append(row_sums(values * upstream))
    stat_tile[...] = jnp.concatenate(rows_of[0] + rows_of[1], 0)
    stats.start()
    every(first, "scatter_mid")
    stats.middle()
    every(first, "scatter_end")
    total = stats.end()
    inverses = 1.0 / jnp.sqrt(total[0:blocks] / D + 1e-05)
    pulls = inverses * inverses * inverses * (total[blocks:2 * blocks] / D)
    line = lax.broadcasted_iota(jnp.int32, (blocks, gains.shape[1]), 0)
    for block in range(blocks):
        here = pl.ds(block * 128, 128)
        pick = jnp.where(line == block, 1.0, 0.0).astype(F32)
        scale = dot(inverses, pick, FIRST, HIGHEST)
        pull = dot(pulls, pick, FIRST, HIGHEST)
        values = stored[here, :]
        inside = pl.ds((block % per_slot) * 128, 128)
        upstream = gains * branch[block // per_slot, inside, :].astype(F32)
        term[here, :] = scale * upstream - values * pull
        normed[here, :] = (values * scale * gains).astype(BF16)
    every(first, "near_end")
    chain.start()
    every(first, "gather_start")
    chain.slot(0)
    every(first, "gather_mid")
    chain.slot(1)

    rows = jnp.zeros((R, gains.shape[1]), F32)
    for index in range(HALVES):
        first[index].gather_end()
        for batch in range(index * per_part, (index + 1) * per_part):
            wide = normed[pl.ds(batch * acts.shape[1], acts.shape[1]), :]
            for piece in split(sum_s[pl.ds(batch * R, R), :], 3):
                rows = rows + dot(piece, wide)
    pieces = split(rows, 2)
    for index in range(HALVES):
        part_q[spans[index], :] = sum(dot(normed[spans[index], :], piece, LAST) for piece in pieces)
        second[index].scatter_start()
    full = dot(rows, rows, LAST, HIGHEST)
    part_g[0:128, 0:128] = full[0:128, 0:128]
    part_g[0:128, 128:256] = full[128:256, 128:256]
    part_g[128:192, 0:128] = full[0:64, 128:256]
    part_g[128:192, 128:256] = full[64:128, 128:256]
    square.start()
    chain.slot(2)
    part_c[...] = sum(dot(piece, basis[...]) for piece in pieces)
    every(second, "scatter_mid")
    square.middle()
    chain.slot(3)
    every(second, "scatter_end")
    square.spread()
    cross.start()
    chain.slot(4)
    every(second, "near_end")
    square.end()
    factor_panel(0, sum_g, inverse, upper)
    cross.middle()
    every(second, "gather_start")
    factor_panel(1, sum_g, inverse, upper)
    cross.spread()
    chain.slot(5)
    factor_panel(2, sum_g, inverse, upper)
    every(second, "gather_mid")
    factor_panel(3, sum_g, inverse, upper)
    chain.slot(6)
    chain.end()
    grad_out[...] = grad[...]
    cross.end()

    mixed = 0.9 * sum(dot(moment[...], piece, LAST) for piece in split(sum_c[...], 2))
    high, low = split(inverse[...], 2)
    for index in range(HALVES):
        second[index].gather_end()
        for batch in range(index * per_part, (index + 1) * per_part):
            for piece in split(sum_q[pl.ds(batch * acts.shape[1], acts.shape[1]), :], 2):
                mixed = mixed + 0.1 * dot(hidden[batch], piece)
    mixed_high, mixed_low = split(mixed, 2)
    moment_out[...] = (dot(mixed_high, high, LAST) + dot(mixed_low, high, LAST)
                       + dot(mixed_high, low, LAST))
    for job in (stats, *first, *second, square, cross, chain):
        job.finish()


def round_kernel(grad, moment, grad_out, moment_out):
    grad_out[...] = grad[...].astype(BF16)
    moment_out[...] = moment[...].astype(BF16)


def rounded(*arrays):
    steps = 4
    specs = [pl.BlockSpec((a.shape[0] // steps, a.shape[1]), lambda i: (i, 0)) for a in arrays]
    return pl.pallas_call(
        round_kernel,
        grid=(steps,),
        out_shape=tuple(jax.ShapeDtypeStruct(a.shape, BF16) for a in arrays),
        in_specs=specs,
        out_specs=tuple(specs),
        name="round_outputs",
    )(*arrays)


def local(acts, act_slot, norm_gain, branch_grad, hidden_grad, sketch_seed, basis_old, moment_old):
    batches, rows, features = acts.shape[1:]
    tokens = batches * rows
    units = hidden_grad.shape[-1]
    chips = lax.axis_size("pipe") // 2
    vmem = pl.BlockSpec(memory_space=pltpu.VMEM)
    smem = pl.BlockSpec(memory_space=pltpu.SMEM)
    dma = pltpu.SemaphoreType.DMA
    tile = (2 * (tokens // 128), 128)
    whole = pltpu.VMEM((tokens, R), F32)
    square = pltpu.VMEM((R, R), F32)
    upper_blocks = pltpu.VMEM((R - PANEL, R), F32)
    wide = pltpu.VMEM((tokens, features), F32)
    half = pltpu.VMEM((tokens // 2, features), F32)
    grad, moment = pl.pallas_call(
        functools.partial(kernel, chips),
        out_shape=(jax.ShapeDtypeStruct((tokens, features), F32),
                   jax.ShapeDtypeStruct((units, R), F32)),
        in_specs=[vmem, smem, vmem, vmem, vmem, vmem, vmem, vmem],
        out_specs=(vmem, vmem),
        scratch_shapes=[
            wide, whole, whole, pltpu.VMEM((tokens, features), BF16), wide, wide, whole, whole,
            upper_blocks, upper_blocks, square, square, square, square,
            pltpu.VMEM(tile, F32), pltpu.VMEM((2, SIDE - 1) + tile, F32), pltpu.VMEM(tile, F32),
            dma((2,)), dma((2,)),
            half, half, wide,
        ] + [dma((CHAIN,))] * 6
        + Reduce.scratch(tokens // HALVES) * (2 * HALVES) + Small.scratch(R - PANEL) + Small.scratch(R),
        compiler_params=pltpu.CompilerParams(collective_id=1, has_side_effects=True,
                                             vmem_limit_bytes=60 * 1024 * 1024),
        name="section_backward",
    )(acts[0], act_slot, norm_gain, branch_grad[0], hidden_grad[0].swapaxes(1, 2),
      sketch_seed, basis_old[0], moment_old[0].T)
    grad, moment = rounded(grad, moment)
    return (grad.reshape(branch_grad.shape), moment.T[None])


def solution(mesh):
    in_specs = (
        P("pipe", None, None, "dp"),
        P("pipe", None),
        P("pipe", "dp"),
        P("pipe", None, None, "dp"),
        P("pipe", None, None, "dp"),
        P("pipe", "dp"),
        P("pipe", "dp", None),
        P("pipe", None, "dp"),
    )
    out_specs = (P("pipe", None, None, "dp"), P("pipe", None, "dp"))
    return jax.shard_map(local, mesh=mesh, in_specs=in_specs, out_specs=out_specs, check_vma=False)
```

```python
import functools

import jax
import jax.numpy as jnp
from jax import lax
from jax.experimental import pallas as pl
from jax.experimental.pallas import tpu as pltpu
from jax.sharding import PartitionSpec as P

D = 16384
R = 256
MESH = pl.DeviceIdType.MESH
HIGHEST = lax.Precision.HIGHEST
F32 = jnp.float32
BF16 = jnp.bfloat16
SIDE = 8
CHAIN = 4
PANEL = 64
GROUP = 8
HALVES = 2
FIRST = ((0,), (0,))
LAST = ((1,), (1,))
PLAIN = ((1,), (0,))


def dot(a, b, contract=PLAIN, precision=None):
    return lax.dot_general(a, b, (contract, ((), ())), precision=precision,
                           preferred_element_type=F32)


def split(value, count):
    parts = []
    for _ in range(count):
        part = value.astype(BF16)
        parts.append(part)
        value = value - part.astype(F32)
    return parts


def row_sums(values):
    ones = jnp.ones((8, values.shape[1]), BF16)
    return sum(dot(ones, piece, LAST) for piece in split(values, 3))[0:1, :]


class Place:
    def __init__(self):
        self.pipe = lax.axis_index("pipe")
        self.dp = lax.axis_index("dp")
        self.y, self.z = self.dp // SIDE, self.dp % SIDE
        self.core = self.pipe % 2
        self.x = self.pipe // 2
        self.turn = 1 - 2 * self.core

    def wrap(self, value):
        return (value + 2 * SIDE) % SIDE

    def along(self, axis, steps):
        if axis == 0:
            return (self.pipe, self.wrap(self.y + steps) * SIDE + self.z)
        return (self.pipe, self.y * SIDE + self.wrap(self.z + steps))

    def at(self, axis):
        return self.y if axis == 0 else self.z


def send(source, target, send_sem, recv_sem, device):
    pltpu.make_async_remote_copy(
        src_ref=source, dst_ref=target, send_sem=send_sem, recv_sem=recv_sem,
        device_id=device, device_id_type=MESH,
    ).start()


def await_bytes(like, sem):
    pltpu.make_async_copy(like, like, sem).wait()


class Reduce:
    def __init__(self, place, x, out, scratch):
        self.p, self.x, self.out = place, x, out
        self.tree, self.total, self.near, self.recv, self.sent = scratch
        self.chunk = x.shape[0] // SIDE
        self.sub = self.chunk // SIDE

    @staticmethod
    def scratch(rows):
        chunk = rows // SIDE
        return [
            pltpu.VMEM((2, 7, chunk, 128), F32),
            pltpu.VMEM((2, chunk, 128), F32),
            pltpu.VMEM((2, SIDE - 1, chunk // SIDE, 128), F32),
            pltpu.SemaphoreType.DMA((2, 8)),
            pltpu.SemaphoreType.DMA((2, 4)),
        ]

    def part(self, ref, half, index):
        rows = pl.ds(pl.multiple_of(index * self.chunk, 8), self.chunk)
        return ref.at[rows, pl.ds(128 * half, 128)]

    def owned(self, half, steps):
        p = self.p
        return p.wrap(p.at(half) + p.turn * steps)

    def tree_send(self, half, source, slot, sem, steps):
        p = self.p
        send(source, self.tree.at[half, slot], self.sent.at[half, 0], self.recv.at[half, sem],
             p.along(half, p.turn * steps))

    def scatter_start(self):
        for owner, slot, sem, steps in ((4, 0, 0, 2), (3, 1, 0, 1), (-3, 2, 1, -1),
                                        (1, 3, 2, 1), (-1, 4, 2, -1)):
            for half in range(2):
                self.tree_send(half, self.part(self.x, half, self.owned(half, owner)),
                               slot, sem, steps)

    def scatter_mid(self):
        for half in range(2):
            await_bytes(self.tree.at[half, 0:2], self.recv.at[half, 0])
            self.tree[half, 0] = (self.tree[half, 0] + self.tree[half, 1]
                                  + self.part(self.x, half, self.owned(half, 2))[...])
            self.tree_send(half, self.tree.at[half, 0], 5, 2, 2)
        for half in range(2):
            await_bytes(self.tree.at[half, 2], self.recv.at[half, 1])
            self.tree[half, 2] = (self.tree[half, 2]
                                  + self.part(self.x, half, self.owned(half, -2))[...])
            self.tree_send(half, self.tree.at[half, 2], 6, 2, -2)

    def scatter_end(self):
        p = self.p
        for half in range(2):
            await_bytes(self.tree.at[half, 3:7], self.recv.at[half, 2])
            value = self.part(self.x, half, p.at(half))[...]
            for slot in range(3, 7):
                value = value + self.tree[half, slot]
            self.total[half] = value
            for steps in (4, 3, 5, 2, 6, 1, 7):
                there = p.wrap(p.at(1 - half) + steps)
                send(self.total.at[half, pl.ds(pl.multiple_of(there * self.sub, 8), self.sub)],
                     self.near.at[half, steps - 1], self.sent.at[half, 1],
                     self.recv.at[half, 3], p.along(1 - half, steps))

    def near_end(self):
        p = self.p
        for half in range(2):
            await_bytes(self.near.at[half], self.recv.at[half, 3])
            value = self.total[half, pl.ds(pl.multiple_of(p.at(1 - half) * self.sub, 8), self.sub)]
            for slot in range(SIDE - 1):
                value = value + self.near[half, slot]
            start = p.at(half) * self.chunk + p.at(1 - half) * self.sub
            place = self.out.at[pl.ds(pl.multiple_of(start, 8), self.sub), pl.ds(128 * half, 128)]
            place[...] = value
            for steps in (4, 3, 5, 2, 6, 1, 7):
                send(place, place, self.sent.at[half, 2], self.recv.at[half, 4],
                     p.along(1 - half, steps))

    def gather_send(self, half, index, sem, steps):
        p = self.p
        place = self.part(self.out, half, index)
        send(place, place, self.sent.at[half, 3], self.recv.at[half, sem],
             p.along(half, p.turn * steps))

    def gather_start(self):
        for half in range(2):
            await_bytes(self.near.at[half], self.recv.at[half, 4])
            for sem, steps in ((5, 2), (6, -2), (7, 1), (7, -1)):
                self.gather_send(half, self.p.at(half), sem, steps)

    def gather_mid(self):
        for half in range(2):
            await_bytes(self.tree.at[half, 0], self.recv.at[half, 5])
            self.gather_send(half, self.owned(half, -2), 7, 2)
            self.gather_send(half, self.owned(half, -2), 7, 1)
        for half in range(2):
            await_bytes(self.tree.at[half, 0], self.recv.at[half, 6])
            self.gather_send(half, self.owned(half, 2), 7, -1)

    def gather_end(self):
        for half in range(2):
            await_bytes(self.tree.at[half, 0:5], self.recv.at[half, 7])

    def finish(self):
        for half in range(2):
            await_bytes(self.tree.at[half], self.sent.at[half, 0])
            await_bytes(self.near.at[half], self.sent.at[half, 1])
            await_bytes(self.near.at[half], self.sent.at[half, 2])
            await_bytes(self.tree.at[half], self.sent.at[half, 3])


class Small:
    def __init__(self, place, x, out, scratch):
        self.p, self.x, self.out = place, x, out
        self.slots, self.mid, self.recv, self.sent = scratch
        self.chunk = x.shape[0] // SIDE

    @staticmethod
    def scratch(rows):
        chunk = rows // SIDE
        return [
            pltpu.VMEM((2, 2, SIDE - 1, chunk, 128), F32),
            pltpu.VMEM((2, chunk, 128), F32),
            pltpu.SemaphoreType.DMA((2, 3)),
            pltpu.SemaphoreType.DMA((2, 3)),
        ]

    def part(self, ref, half, index):
        rows = pl.ds(pl.multiple_of(index * self.chunk, 8), self.chunk)
        return ref.at[rows, pl.ds(128 * half, 128)]

    def start(self):
        p = self.p
        for steps in (4, 3, 5, 2, 6, 1, 7):
            for half in range(2):
                send(self.part(self.x, half, p.wrap(p.at(half) + steps)),
                     self.slots.at[0, half, steps - 1], self.sent.at[half, 0],
                     self.recv.at[half, 0], p.along(half, steps))

    def total(self, stage, half, value):
        await_bytes(self.slots.at[stage, half], self.recv.at[half, stage])
        for slot in range(SIDE - 1):
            value = value + self.slots[stage, half, slot]
        return value

    def middle(self):
        p = self.p
        for half in range(2):
            self.mid[half] = self.total(0, half, self.part(self.x, half, p.at(half))[...])
            for steps in (4, 3, 5, 2, 6, 1, 7):
                send(self.mid.at[half], self.slots.at[1, half, steps - 1], self.sent.at[half, 1],
                     self.recv.at[half, 1], p.along(1 - half, steps))

    def spread(self):
        p = self.p
        for half in range(2):
            place = self.part(self.out, half, p.at(half))
            place[...] = self.total(1, half, self.mid[half])
            for steps in (4, 3, 5, 2, 6, 1, 7):
                send(place, place, self.sent.at[half, 2], self.recv.at[half, 2],
                     p.along(half, steps))

    def end(self):
        for half in range(2):
            await_bytes(self.slots.at[0, half], self.recv.at[half, 2])

    def finish(self):
        for half in range(2):
            for stage in range(3):
                await_bytes(self.slots.at[0, half], self.sent.at[half, stage])


class Stats:
    def __init__(self, place, tile, slots, mid, recv, sent):
        self.p, self.tile, self.slots, self.mid = place, tile, slots, mid
        self.recv, self.sent = recv, sent

    def push(self, source, axis):
        for steps in (4, 3, 5, 2, 6, 1, 7):
            send(source, self.slots.at[axis, steps - 1], self.sent.at[axis], self.recv.at[axis],
                 self.p.along(axis, steps))

    def total(self, source, axis):
        await_bytes(self.slots.at[axis], self.recv.at[axis])
        value = source[...]
        for slot in range(SIDE - 1):
            value = value + self.slots[axis, slot]
        return value

    def start(self):
        self.push(self.tile, 0)

    def middle(self):
        self.mid[...] = self.total(self.tile, 0)
        self.push(self.mid, 1)

    def end(self):
        return self.total(self.mid, 1)

    def finish(self):
        for axis in range(2):
            await_bytes(self.slots.at[axis], self.sent.at[axis])


class Chain:
    def __init__(self, place, chips, term, grad, other, above, held, sems):
        self.p, self.chips = place, chips
        self.term, self.grad, self.other, self.above, self.held = term, grad, other, above, held
        self.pair_s, self.pair_r, self.down_s, self.down_r, self.give_s, self.give_r = sems
        self.half_rows = term.shape[0] // 2
        self.size = self.half_rows // CHAIN
        self.partner, self.upper, self.lower = chain_peers(place, chips)

    def rows(self, core, index):
        return pl.ds(pl.multiple_of(core * self.half_rows + index * self.size, 8), self.size)

    def remote(self, source, target, send_sem, recv_sem, device):
        return pltpu.make_async_remote_copy(
            src_ref=source, dst_ref=target, send_sem=send_sem, recv_sem=recv_sem,
            device_id=device, device_id_type=MESH)

    def pair(self, index):
        here = pl.ds(index * self.size, self.size)
        return self.remote(self.term.at[self.rows(1 - self.p.core, index)], self.other.at[here],
                           self.pair_s.at[index], self.pair_r.at[index], self.partner)

    def down(self, index):
        here = pl.ds(index * self.size, self.size)
        return self.remote(self.held.at[here], self.above.at[here],
                           self.down_s.at[index], self.down_r.at[index], self.lower)

    def give(self, index):
        here = pl.ds(self.half_rows + index * self.size, self.size)
        return self.remote(self.held.at[here], self.grad.at[self.rows(self.p.core, index)],
                           self.give_s.at[index], self.give_r.at[index], self.partner)

    def start(self):
        for index in range(CHAIN):
            self.pair(index).start()

    def slot(self, slot):
        for shift in range(self.chips):
            index = slot - shift
            if 0 <= index < CHAIN:
                @pl.when(self.p.x == self.chips - 1 - shift)
                def _():
                    here = pl.ds(index * self.size, self.size)
                    self.pair(index).wait_recv()
                    own_sum = self.term[self.rows(self.p.core, index)]
                    mate = self.other[here]
                    mate_sum = mate
                    if shift > 0:
                        self.down(index).wait_recv()
                        own_sum = own_sum + self.above[here]
                        mate_sum = mate + self.above[here]
                    both = own_sum + mate
                    lead = self.p.core == 0
                    self.held[here] = both
                    self.held[pl.ds(self.half_rows + index * self.size, self.size)] = jnp.where(
                        lead, mate_sum, both)
                    self.grad[self.rows(self.p.core, index)] = jnp.where(lead, both, own_sum)
                    if shift < self.chips - 1:
                        self.down(index).start()
                    self.give(index).start()

    def end(self):
        for index in range(CHAIN):
            place = self.grad.at[self.rows(1 - self.p.core, index)]
            await_bytes(place, self.give_r.at[index])

    def finish(self):
        for index in range(CHAIN):
            self.pair(index).wait_send()
            self.give(index).wait_send()

        @pl.when(self.p.x > 0)
        def _():
            for index in range(CHAIN):
                self.down(index).wait_send()


def chain_peers(p, chips):
    return ((p.x * 2 + 1 - p.core, p.dp),
            (((p.x + 1) % chips) * 2 + p.core, p.dp),
            (((p.x + chips - 1) % chips) * 2 + p.core, p.dp))


def eliminate(value, width, row):
    for k in range(0, width, GROUP):
        columns = [jnp.broadcast_to(value[:, k + j:k + j + 1], value.shape) for j in range(GROUP)]
        scales, low, uppers, weights = [], {}, [], []
        for j in range(GROUP):
            pivot = columns[j][k + j:k + j + 1, :]
            for m in range(j):
                pivot = pivot - low[j, m] * low[j, m]
            scales.append(lax.rsqrt(pivot))
            for i in range(j + 1, GROUP):
                entry = columns[j][k + i:k + i + 1, :]
                for m in range(j):
                    entry = entry - low[i, m] * low[j, m]
                low[i, j] = entry * scales[j]
        for j in range(GROUP):
            upper, weight = value[k + j:k + j + 1, :], columns[j]
            for m in range(j):
                upper = upper - low[j, m] * uppers[m]
                weight = weight - weights[m] * low[j, m]
            uppers.append(upper * scales[j])
            weights.append(weight * scales[j])
        updated = value
        for j in range(GROUP):
            updated = updated - weights[j] * uppers[j]
        for j in range(GROUP):
            updated = jnp.where(row == k + j, uppers[j], updated)
        value = jnp.where(row < k, value, updated)
    return value


def gram_rows(panel, gram):
    if panel < 2:
        right = gram[128:192, 128 * panel:128 * panel + 128]
        return jnp.concatenate([gram[PANEL * panel:PANEL * (panel + 1), 0:128], right], 1)
    right = gram[PANEL * (panel - 2):PANEL * (panel - 1), 128:256]
    return jnp.concatenate([jnp.zeros((PANEL, 128), F32), right], 1)


def factor_panel(panel, gram, inverse, upper):
    width = PANEL
    start = panel * width
    here = pl.ds(start, width)
    row = lax.broadcasted_iota(jnp.int32, (width, 128), 0)
    lane = lax.broadcasted_iota(jnp.int32, (width, 128), 1)
    block = gram_rows(panel, gram)
    wide = lax.broadcasted_iota(jnp.int32, (width, R), 1)
    deep = lax.broadcasted_iota(jnp.int32, (width, R), 0)
    target = jnp.where(wide == deep + start, 1.0, 0.0).astype(F32)
    if panel > 0:
        before = upper[0:start, :]
        left = before[:, start:start + width]
        block = block - dot(left, before, FIRST, HIGHEST)
        target = target - dot(left, inverse[0:start, :], FIRST, HIGHEST)
    tile = block[:, 128 * (start // 128):128 * (start // 128) + 128]
    shift = start % 128
    if shift:
        tile = pltpu.roll(tile, 128 - shift, 1)
    value = jnp.where(lane < width, tile, jnp.where(lane == row + width, 1.0, 0.0).astype(F32))
    value = eliminate(value, width, row)
    corner = value[:, width:2 * width]
    upper[here, :] = dot(corner, block, PLAIN, HIGHEST)
    inverse[here, :] = dot(corner, target, PLAIN, HIGHEST)


def kernel(chips, acts, slots, gain, branch, hidden, seed, basis, moment, grad_out, moment_out,
           stored, part_s, sum_s, normed, term, grad, part_q, sum_q, part_g, sum_g, part_c, sum_c,
           inverse, upper, stat_tile, stat_slots, stat_mid, stat_recv, stat_sent,
           other, above, held, *rest):
    rest = list(rest)
    chain_sems = [rest.pop(0) for _ in range(6)]
    firsts = [[rest.pop(0) for _ in range(5)] for _ in range(HALVES)]
    seconds = [[rest.pop(0) for _ in range(5)] for _ in range(HALVES)]
    scratch = [[rest.pop(0) for _ in range(4)] for _ in range(2)]
    p = Place()
    tokens = stored.shape[0]
    blocks = tokens // 128
    per_part = hidden.shape[0] // HALVES

    barrier = pltpu.get_barrier_semaphore()
    peers = [p.along(axis, steps) for axis in range(2) for steps in range(1, SIDE)]
    peers += list(chain_peers(p, chips))
    for peer in peers:
        pl.semaphore_signal(barrier, inc=1, device_id=peer, device_id_type=MESH)

    count = lax.broadcasted_iota(jnp.int32, (R, seed.shape[1]), 0).astype(F32) + 1.0
    product = seed[...].astype(F32) * count
    levels = product - jnp.floor(product * (1.0 / 65521.0)) * 65521.0
    levels = jnp.where(levels < 0.0, levels + 65521.0, levels)
    levels = jnp.where(levels >= 65521.0, levels - 65521.0, levels)
    omega = ((levels - 32760.0) * (1.7320508 / 32760.0)).astype(BF16)

    def sketch_share(index):
        for batch in range(index * per_part, (index + 1) * per_part):
            part_s[pl.ds(batch * R, R), :] = dot(omega, hidden[batch])

    sketch_share(0)
    pl.semaphore_wait(barrier, len(peers))

    stats = Stats(p, stat_tile, stat_slots, stat_mid, stat_recv, stat_sent)
    share = tokens // HALVES
    spans = [pl.ds(index * share, share) for index in range(HALVES)]
    first = [Reduce(p, part_s.at[span], sum_s.at[span], own) for span, own in zip(spans, firsts)]
    second = [Reduce(p, part_q.at[span], sum_q.at[span], own) for span, own in zip(spans, seconds)]
    square = Small(p, part_g, sum_g, scratch[0])
    cross = Small(p, part_c, sum_c, scratch[1])
    chain = Chain(p, chips, term, grad, other, above, held, chain_sems)

    def every(jobs, step):
        for job in jobs:
            getattr(job, step)()

    first[0].scatter_start()
    for index in range(1, HALVES):
        sketch_share(index)
        first[index].scatter_start()
    gains = gain[...].astype(F32)
    per_slot = acts.shape[1] // 128
    rows_of = [[], []]
    for block in range(blocks):
        here = pl.ds((block % per_slot) * 128, 128)
        values = acts[slots[0, block // per_slot], here, :].astype(F32)
        stored[pl.ds(block * 128, 128), :] = values
        upstream = gains * branch[block // per_slot, here, :].astype(F32)
        rows_of[0].append(row_sums(values * values))
        rows_of[1].append(row_sums(values * upstream))
    stat_tile[...] = jnp.concatenate(rows_of[0] + rows_of[1], 0)
    stats.start()
    every(first, "scatter_mid")
    stats.middle()
    every(first, "scatter_end")
    total = stats.end()
    inverses = 1.0 / jnp.sqrt(total[0:blocks] / D + 1e-05)
    pulls = inverses * inverses * inverses * (total[blocks:2 * blocks] / D)
    line = lax.broadcasted_iota(jnp.int32, (blocks, gains.shape[1]), 0)
    for block in range(blocks):
        here = pl.ds(block * 128, 128)
        pick = jnp.where(line == block, 1.0, 0.0).astype(F32)
        scale = dot(inverses, pick, FIRST, HIGHEST)
        pull = dot(pulls, pick, FIRST, HIGHEST)
        values = stored[here, :]
        inside = pl.ds((block % per_slot) * 128, 128)
        upstream = gains * branch[block // per_slot, inside, :].astype(F32)
        term[here, :] = scale * upstream - values * pull
        normed[here, :] = (values * scale * gains).astype(BF16)
    every(first, "near_end")
    chain.start()
    every(first, "gather_start")
    chain.slot(0)
    every(first, "gather_mid")
    chain.slot(1)

    rows = jnp.zeros((R, gains.shape[1]), F32)
    for index in range(HALVES):
        first[index].gather_end()
        for batch in range(index * per_part, (index + 1) * per_part):
            wide = normed[pl.ds(batch * acts.shape[1], acts.shape[1]), :]
            for piece in split(sum_s[pl.ds(batch * R, R), :], 3):
                rows = rows + dot(piece, wide)
    pieces = split(rows, 2)
    for index in range(HALVES):
        part_q[spans[index], :] = sum(dot(normed[spans[index], :], piece, LAST) for piece in pieces)
        second[index].scatter_start()
    full = dot(rows, rows, LAST, HIGHEST)
    part_g[0:128, 0:128] = full[0:128, 0:128]
    part_g[0:128, 128:256] = full[128:256, 128:256]
    part_g[128:192, 0:128] = full[0:64, 128:256]
    part_g[128:192, 128:256] = full[64:128, 128:256]
    square.start()
    chain.slot(2)
    part_c[...] = sum(dot(piece, basis[...]) for piece in pieces)
    every(second, "scatter_mid")
    square.middle()
    chain.slot(3)
    every(second, "scatter_end")
    square.spread()
    cross.start()
    chain.slot(4)
    every(second, "near_end")
    square.end()
    factor_panel(0, sum_g, inverse, upper)
    cross.middle()
    factor_panel(1, sum_g, inverse, upper)
    every(second, "gather_start")
    factor_panel(2, sum_g, inverse, upper)
    cross.spread()
    chain.slot(5)
    factor_panel(3, sum_g, inverse, upper)
    every(second, "gather_mid")
    chain.slot(6)
    chain.end()
    grad_out[...] = grad[...]
    cross.end()

    mixed = 0.9 * sum(dot(moment[...], piece, LAST) for piece in split(sum_c[...], 2))
    high, low = split(inverse[...], 2)
    for index in range(HALVES):
        second[index].gather_end()
        for batch in range(index * per_part, (index + 1) * per_part):
            for piece in split(sum_q[pl.ds(batch * acts.shape[1], acts.shape[1]), :], 2):
                mixed = mixed + 0.1 * dot(hidden[batch], piece)
    mixed_high, mixed_low = split(mixed, 2)
    moment_out[...] = (dot(mixed_high, high, LAST) + dot(mixed_low, high, LAST)
                       + dot(mixed_high, low, LAST))
    for job in (stats, *first, *second, square, cross, chain):
        job.finish()


def round_kernel(grad, moment, grad_out, moment_out):
    grad_out[...] = grad[...].astype(BF16)
    moment_out[...] = moment[...].astype(BF16)


def rounded(*arrays):
    steps = 4
    specs = [pl.BlockSpec((a.shape[0] // steps, a.shape[1]), lambda i: (i, 0)) for a in arrays]
    return pl.pallas_call(
        round_kernel,
        grid=(steps,),
        out_shape=tuple(jax.ShapeDtypeStruct(a.shape, BF16) for a in arrays),
        in_specs=specs,
        out_specs=tuple(specs),
        name="round_outputs",
    )(*arrays)


def local(acts, act_slot, norm_gain, branch_grad, hidden_grad, sketch_seed, basis_old, moment_old):
    batches, rows, features = acts.shape[1:]
    tokens = batches * rows
    units = hidden_grad.shape[-1]
    chips = lax.axis_size("pipe") // 2
    vmem = pl.BlockSpec(memory_space=pltpu.VMEM)
    smem = pl.BlockSpec(memory_space=pltpu.SMEM)
    dma = pltpu.SemaphoreType.DMA
    tile = (2 * (tokens // 128), 128)
    whole = pltpu.VMEM((tokens, R), F32)
    square = pltpu.VMEM((R, R), F32)
    upper_blocks = pltpu.VMEM((R - PANEL, R), F32)
    wide = pltpu.VMEM((tokens, features), F32)
    half = pltpu.VMEM((tokens // 2, features), F32)
    grad, moment = pl.pallas_call(
        functools.partial(kernel, chips),
        out_shape=(jax.ShapeDtypeStruct((tokens, features), F32),
                   jax.ShapeDtypeStruct((units, R), F32)),
        in_specs=[vmem, smem, vmem, vmem, vmem, vmem, vmem, vmem],
        out_specs=(vmem, vmem),
        scratch_shapes=[
            wide, whole, whole, pltpu.VMEM((tokens, features), BF16), wide, wide, whole, whole,
            upper_blocks, upper_blocks, square, square, square, square,
            pltpu.VMEM(tile, F32), pltpu.VMEM((2, SIDE - 1) + tile, F32), pltpu.VMEM(tile, F32),
            dma((2,)), dma((2,)),
            half, half, wide,
        ] + [dma((CHAIN,))] * 6
        + Reduce.scratch(tokens // HALVES) * (2 * HALVES) + Small.scratch(R - PANEL) + Small.scratch(R),
        compiler_params=pltpu.CompilerParams(collective_id=1, has_side_effects=True,
                                             vmem_limit_bytes=60 * 1024 * 1024),
        name="section_backward",
    )(acts[0], act_slot, norm_gain, branch_grad[0], hidden_grad[0].swapaxes(1, 2),
      sketch_seed, basis_old[0], moment_old[0].T)
    grad, moment = rounded(grad, moment)
    return (grad.reshape(branch_grad.shape), moment.T[None])


def solution(mesh):
    in_specs = (
        P("pipe", None, None, "dp"),
        P("pipe", None),
        P("pipe", "dp"),
        P("pipe", None, None, "dp"),
        P("pipe", None, None, "dp"),
        P("pipe", "dp"),
        P("pipe", "dp", None),
        P("pipe", None, "dp"),
    )
    out_specs = (P("pipe", None, None, "dp"), P("pipe", None, "dp"))
    return jax.shard_map(local, mesh=mesh, in_specs=in_specs, out_specs=out_specs, check_vma=False)
```
